32 devices in a mesh: design: 4 (over x, core), graph: 8 (over z, y).
Axes of the slice: x: 2, y: 2, z: 4, core: 2. Of those that a mesh axis runs over, the one named last changes fastest.
Arguments:
- nodes: bfloat16 [4, 65536, 128], P('design', 'graph'), may hold values from -6 to 6
- adjacency: bfloat16 [4, 512, 4, 128, 128], P('design', 'graph'), may hold values from -0.25 to 0.25
- tile_src: int32 [4, 512, 4], P('design', 'graph'), may hold values from 0 to 67, as said below
- pool_dst: int32 [4, 512, 1], P('design', 'graph'), may hold values from 0 to 7; in each aligned block of 64 rows (0 to 63, 64 to 127, ..., all dimensions but the last counted through in order) at most 16 rows name the same one
- pool_weight: bfloat16 [4, 512, 128, 128], P('design', 'graph'), may hold values from -0.0625 to 0.0625
- coarse_cot: bfloat16 [4, 1024, 128], P('design', 'graph'), may hold values from -48 to 48
- w_msg: bfloat16 [128, 128], replicated, may hold values from -0.5 to 0.5
- w_in: bfloat16 [256, 128], replicated, may hold values from -0.375 to 0.375
- b_in: float32 [128], replicated, may hold values from -3 to 3
- w_out: bfloat16 [128, 128], replicated, may hold values from -0.5 to 0.5
Outputs:
- fine_out: bfloat16 [4, 65536, 128], P('design', 'graph')
- coarse: bfloat16 [4, 1024, 128], P('design', 'graph')
- grad_msg: float32 [128, 128], replicated
- grad_in: float32 [256, 128], replicated
- grad_bias: float32 [128], replicated
- grad_out: float32 [128, 128], replicated
The draws below stay inside these ranges and needn't reach their ends.
Inputs may be any that keep to these rules, and one draw needn't show every extreme that they name: `tile_src`: entry 0 is the destination tile itself (its slab index plus 2); every entry lies within 2 tiles of the destination tile; each slab's first and last tiles list the outermost neighbouring tile. `pool_dst`: among the 64 fine tiles of one slab, at most 16 name the same coarse tile.
All inputs are finite; a program needn't handle non-finite values.
Results may differ from the reference program's by a relative error of at most 0.0067.
Values may be sent and summed in bfloat16 or wider, within the bound.
No kernel may reach another device: no remote copies, remote signals or barrier semaphores. Data moves between devices by JAX's collectives and lax.ppermute only.
A program may use at most 128 MiB of HBM per device.

```python
import math
import jax
import jax.numpy as jnp
import numpy as np
from jax import lax

H = 128
TILE = 128
NBR = 4
HT = 2
TPD = 64
CAP = 16
DESIGNS = 4
GRAPH_TILES = 512
NODES = 65536
COARSE_ROWS = 1024
N_GRAPH = 8


def draw_tile_src(key, part):
    offsets = jax.random.randint(key, (DESIGNS, GRAPH_TILES, NBR), -HT, HT + 1)
    local = (jnp.arange(GRAPH_TILES) % TPD)[None, :, None]
    slot = jnp.arange(NBR)[None, None, :]
    source = local + HT + jnp.where(slot == 0, 0, offsets)
    source = jnp.where((slot == 1) & (local == 0), 0, source)
    source = jnp.where((slot == 1) & (local == TPD - 1), TPD + 2 * HT - 1, source)
    return source.astype(jnp.int32)


def block_levels(own_key, extent, pieces, low, high):
    level, own = 1.0, jax.random.fold_in(own_key, 6)
    for dim, shards_of in pieces:
        steps = jnp.exp(jax.random.uniform(jax.random.fold_in(own, dim), (shards_of,), jnp.float32, low / len(pieces), high / len(pieces)))
        level = level * jnp.repeat(steps, extent[dim] // shards_of).reshape([-1 if axis == dim else 1 for axis in range(len(extent))])
    return level


def assign_block(key, own, number, rows, count, top, reach, skew):
    order = jax.random.permutation(key, count)
    heavy_load, usual = load_shares(count, rows * top, reach, skew, True), load_shares(count, rows * top, reach, skew, False)
    places = jnp.arange(count)

    def named(lengths, offset_by):
        used = int((lengths > 0).sum())
        fixed = max(1, used // 4)
        moved = fixed + (places - fixed + offset_by * (used - fixed)) % max(1, count - fixed)
        return jnp.zeros((count,), jnp.int32).at[order[jnp.where(places < fixed, places, moved)]].set(jnp.asarray(lengths, jnp.int32))

    lengths = jnp.where(number % 4 == 0, named(heavy_load, number // 4), named(usual, number - number // 4 - 1))
    mixed = jax.random.permutation(jax.random.fold_in(own, 3), count)
    giver, sink = mixed[0:count // 2 * 2:2], mixed[1:count // 2 * 2:2]
    slack = jnp.minimum(lengths[giver] - 1, reach - lengths[sink]) // 2
    slack = jnp.where((giver == order[0]) | (sink == order[0]) | (lengths[sink] == 0), 0, jnp.maximum(slack, 0))
    moved = jax.random.randint(jax.random.fold_in(own, 4), (count // 2,), 0, 1 << 20) % (slack + 1)
    lengths = lengths.at[giver].add(-moved).at[sink].add(moved)
    items = jnp.searchsorted(jnp.cumsum(lengths), jnp.arange(rows * top), side="right").astype(jnp.int32)
    grid = items.reshape(top, rows).T
    grid = grid[jax.random.permutation(jax.random.fold_in(own, 1), rows)]
    offset_by = jax.random.randint(jax.random.fold_in(own, 2), (rows, 1), 0, top)
    return jnp.take_along_axis(grid, (jnp.arange(top)[None, :] + offset_by) % top, axis=1)


def load_shares(amount, total, bound, slope, full):
    weights = [(1 << 20) // math.isqrt(standing ** slope) + 1 for standing in range(1, amount + 1)]
    largest = bound if full else min(bound, max(-(-total // amount), total * weights[0] // sum(weights)))
    least = 1 if total - largest >= amount - 1 else 0
    counts, spare = [largest] + [least] * (amount - 1), total - largest - least * (amount - 1)
    while spare > 0:
        movable = [i for i in range(1, amount) if counts[i] < largest] or [i for i in range(1, amount) if counts[i] < bound]
        pool, left = sum([weights[i] for i in movable]), spare
        for i in movable:
            extra = min(bound - counts[i], max(1, left * weights[i] // pool), spare)
            counts[i] = counts[i] + extra
            spare = spare - extra
    return np.array(counts)


def bell_draw(stream_key, shape, width, limit, shards=(), dtype=jnp.bfloat16):
    drawn = jax.random.normal(stream_key, shape, jnp.float32) * width
    if len(shards) > 0:
        drawn = block_levels(stream_key, shape, shards, -0.22, 0.18) * drawn
    return jnp.clip(drawn, min=-limit, max=limit).astype(dtype)


def setup_inputs(seed: int = 0) -> dict:
    splits = jax.random.split(jax.random.key(seed), 11)
    nodes = bell_draw(splits[0], (DESIGNS, NODES, H), 1.0, 6.0, ((0, 4), (1, 8)))
    adjacency = bell_draw(splits[1], (DESIGNS, GRAPH_TILES, NBR, TILE, TILE), (TILE * NBR) ** -0.5, 0.25, ((0, 4), (1, 8)))
    tile_src = draw_tile_src(jax.random.fold_in(splits[10], 71), 0)
    pool_dst_keys = jax.random.split(jax.random.fold_in(splits[3], 1), DESIGNS * GRAPH_TILES // TPD)
    pool_dst_turns = jax.random.permutation(jax.random.fold_in(splits[3], 3), DESIGNS * GRAPH_TILES // TPD)
    pool_dst = jax.vmap(lambda own, number: assign_block(jax.random.fold_in(splits[3], 2), own, number, TPD, N_GRAPH, 1, CAP, 2))(pool_dst_keys, pool_dst_turns).reshape((DESIGNS, GRAPH_TILES, 1))
    pool_weight = bell_draw(splits[4], (DESIGNS, GRAPH_TILES, TILE, TILE), (TILE * TPD) ** -0.5, 0.0625, ((0, 4), (1, 8)))
    coarse_cot = bell_draw(splits[5], (DESIGNS, COARSE_ROWS, H), 8.0, 48.0, ((0, 4), (1, 8)))
    w_msg = bell_draw(splits[6], (H, H), H ** -0.5, 0.5)
    w_in = bell_draw(splits[7], (2 * H, H), (2 * H) ** -0.5, 0.375)
    b_in = bell_draw(splits[8], (H,), 0.5, 3.0, (), jnp.float32)
    w_out = bell_draw(splits[9], (H, H), H ** -0.5, 0.5)
    return {"nodes": nodes, "adjacency": adjacency, "tile_src": tile_src, "pool_dst": pool_dst, "pool_weight": pool_weight, "coarse_cot": coarse_cot, "w_msg": w_msg, "w_in": w_in, "b_in": b_in, "w_out": w_out}


def silu_slope(pre):
    sig = jax.nn.sigmoid(pre)
    return sig * (1.0 + pre * (1.0 - sig))

def one_design(items, w_msg, w_in, b_in, w_out):
    nodes, adjacency, tile_src, pool_dst, pool_weight, coarse_cot = items
    count = TPD * N_GRAPH
    messages = jnp.dot(nodes, w_msg, preferred_element_type=jnp.float32).astype(jnp.bfloat16)
    tiles = messages.reshape(count, TILE, H)
    blank = jnp.zeros((HT, TILE, H), jnp.bfloat16)
    padded = jnp.concatenate([blank, tiles, blank], axis=0)
    base = (jnp.arange(count) // TPD * TPD).astype(jnp.int32)
    index = base[:, None] + tile_src.astype(jnp.int32)
    agg = jnp.zeros((count, TILE, H), jnp.float32)
    for slot in range(NBR):
        agg = agg + jnp.einsum('tij,tjh->tih', adjacency[:, slot].astype(jnp.float32), padded[index[:, slot]].astype(jnp.float32))
    agg_b = agg.astype(jnp.bfloat16).reshape(NODES, H)
    pre = jnp.dot(nodes, w_in[:H], preferred_element_type=jnp.float32) + jnp.dot(agg_b, w_in[H:], preferred_element_type=jnp.float32) + b_in
    act = jax.nn.silu(pre).astype(jnp.bfloat16)
    fine = (nodes.astype(jnp.float32) + jnp.dot(act, w_out, preferred_element_type=jnp.float32)).astype(jnp.bfloat16)
    contrib = jnp.einsum('tij,tjh->tih', pool_weight.astype(jnp.float32), fine.reshape(count, TILE, H).astype(jnp.float32)).astype(jnp.bfloat16)
    target = pool_dst[:, 0]
    owner_of = (target[None, :] == jnp.arange(N_GRAPH)[:, None]).astype(jnp.float32)
    coarse = jnp.einsum('ot,tih->oih', owner_of, contrib.astype(jnp.float32)).astype(jnp.bfloat16).reshape(N_GRAPH * TILE, H)
    chosen = coarse_cot.reshape(N_GRAPH, TILE, H)[target]
    grad_y = jnp.einsum('tji,tjh->tih', pool_weight.astype(jnp.float32), chosen.astype(jnp.float32)).astype(jnp.bfloat16).reshape(NODES, H)
    grad_out = jnp.dot(act.T, grad_y, preferred_element_type=jnp.float32)
    grad_act = jnp.dot(grad_y, w_out.T, preferred_element_type=jnp.float32)
    grad_pre = (grad_act * silu_slope(pre)).astype(jnp.bfloat16)
    grad_in = jnp.concatenate([jnp.dot(nodes.T, grad_pre, preferred_element_type=jnp.float32), jnp.dot(agg_b.T, grad_pre, preferred_element_type=jnp.float32)], axis=0)
    grad_bias = lax.optimization_barrier(jnp.sum(grad_pre.astype(jnp.float32), axis=0))
    grad_agg = jnp.dot(grad_pre, w_in[H:].T, preferred_element_type=jnp.float32).astype(jnp.bfloat16).reshape(count, TILE, H)
    grad_padded = jnp.zeros((count + 2 * HT, TILE, H), jnp.float32)
    for slot in range(NBR):
        term = jnp.einsum('tij,tih->tjh', adjacency[:, slot].astype(jnp.float32), grad_agg.astype(jnp.float32))
        grad_padded = grad_padded.at[index[:, slot]].add(term)
    grad_m = grad_padded[HT:HT + count].astype(jnp.bfloat16).reshape(NODES, H)
    grad_msg = jnp.dot(nodes.T, grad_m, preferred_element_type=jnp.float32)
    return (fine, coarse, grad_msg, grad_in, grad_bias, grad_out)

def reference(nodes, adjacency, tile_src, pool_dst, pool_weight, coarse_cot, w_msg, w_in, b_in, w_out):

    def step(items):
        return one_design(items, w_msg, w_in, b_in, w_out)
    fine, coarse, grad_msg, grad_in, grad_bias, grad_out = lax.map(step, (nodes, adjacency, tile_src, pool_dst, pool_weight, coarse_cot))
    scale = 1.0 / math.sqrt(DESIGNS * NODES)
    return (fine, coarse, lax.optimization_barrier(jnp.sum(grad_msg, 0)) * scale, lax.optimization_barrier(jnp.sum(grad_in, 0)) * scale, lax.optimization_barrier(jnp.sum(grad_bias, 0)) * scale, lax.optimization_barrier(jnp.sum(grad_out, 0)) * scale)
```

```python
import math

import jax
import jax.numpy as jnp
from jax import lax
from jax.experimental import pallas as pl
from jax.experimental.pallas import tpu as pltpu
from jax.sharding import PartitionSpec as P

H = 128
TILE = 128
NBR = 4
HT = 2
STEPS = 8
F32 = jnp.float32
BF16 = jnp.bfloat16


def dot(a, b, ca=1, cb=0):
    return lax.dot_general(a, b, (((ca,), (cb,)), ((), ())), preferred_element_type=F32)


def split(x):
    hi = x.astype(BF16)
    return hi, (x - hi.astype(F32)).astype(BF16)


def bit_order(count):
    bits = count.bit_length() - 1
    return [sum(((q >> b) & 1) << (bits - 1 - b) for b in range(bits)) for q in range(count)]


def exchange(x, axis, mask):
    return lax.ppermute(x, axis, [(i, i ^ mask) for i in range(lax.axis_size(axis))])


def forward_tiles(per, first, src, dst, me, ext, adj, pw, wcat, bias, a_out, d_out, acc):
    rows = per * TILE
    for j in range(per):
        t = first + j
        picked = [
            ext[pl.ds(pl.multiple_of(src[t, k] * TILE, TILE), TILE), :] for k in range(NBR)
        ]
        weights = jnp.concatenate([adj[j, k] for k in range(NBR)], axis=1)
        summed = dot(weights, jnp.concatenate(picked, axis=0))
        a_out[pl.ds(j * TILE, TILE), :] = summed.astype(BF16)
    own = ext[pl.ds(pl.multiple_of((first + HT) * TILE, TILE), rows), :]
    both = jnp.concatenate([own, a_out[...]], axis=1)
    pre = dot(both, wcat[...]) + bias[...]
    sig = 0.5 * jnp.tanh(0.5 * pre) + 0.5
    act = (pre * sig).astype(BF16)
    d_out[...] = sig * (1.0 + pre * (1.0 - sig))
    for j in range(per):
        part = slice(j * TILE, (j + 1) * TILE)
        term = dot(pw[j], jnp.concatenate([own[part], act[part]], axis=1))
        slot = dst[first + j, 0] ^ me
        acc[slot] += term


def join_weights(w_msg, w_in, wcat):
    wcat[:H] = w_in[:H]
    wcat[H:] = dot(w_msg[...], w_in[H:]).astype(BF16)


def inner_kernel(
    per, base, src, dst, nodes, adj, pw, w_msg, w_in, bias, a_out, d_out, acc, ext, wcat, sem
):
    i = pl.program_id(0)
    me = lax.axis_index("graph")
    total = nodes.shape[0]

    @pl.when(i == 0)
    def _():
        copy = pltpu.make_async_copy(nodes, ext.at[pl.ds(HT * TILE, total)], sem)
        copy.start()
        join_weights(w_msg, w_in, wcat)
        acc[...] = jnp.zeros_like(acc)
        copy.wait()

    forward_tiles(
        per, (base + i) * per, src, dst, me, ext, adj, pw, wcat, bias, a_out, d_out, acc
    )


def outer_kernel(
    per, steps, order, src, dst, nodes, near, far, adj, pw, w_msg, w_in, bias, w_out,
    acc_in, a_in, d_in, a_out, d_out, p_out, send, keep, ext, wcat, acc, sem,
):
    i = pl.program_id(0)
    me = lax.axis_index("graph")
    total = nodes.shape[0]
    margin = HT * TILE

    @pl.when(i == 0)
    def _():
        odd = me & 1
        right = margin + total
        near_at = pl.multiple_of((1 - odd) * right, TILE)
        far_at = pl.multiple_of(odd * right, TILE)
        copies = [
            pltpu.make_async_copy(nodes, ext.at[pl.ds(margin, total)], sem.at[0]),
            pltpu.make_async_copy(near, ext.at[pl.ds(near_at, margin)], sem.at[1]),
            pltpu.make_async_copy(far, ext.at[pl.ds(far_at, margin)], sem.at[2]),
        ]
        for copy in copies:
            copy.start()
        join_weights(w_msg, w_in, wcat)
        acc[...] = acc_in[...]
        for copy in copies:
            copy.wait()

    block = outer_block(i, steps)
    forward_tiles(per, block * per, src, dst, me, ext, adj, pw, wcat, bias, a_out, d_out, acc)

    @pl.when(i == pl.num_programs(0) - 1)
    def _():
        count = len(order)
        for q, r in enumerate(order):
            p_sum = acc[r, :, H:]
            p_out[r] = p_sum
            hi, lo = split(p_sum)
            whole = acc[r, :, :H] + dot(hi, w_out[...]) + dot(lo, w_out[...])
            if q < count // 2:
                keep[q] = whole
            else:
                send[q - count // 2] = whole.astype(BF16)


def outer_block(i, steps):
    return jnp.where(i < steps // 4, i, i + steps // 2)


def backward_kernel(per, levels, dst, *refs):
    cots = refs[:levels]
    nodes, a_in, d_in, pw, p_in, w_out, out, cot_w, total = refs[levels:]
    i = pl.program_id(0)
    me = lax.axis_index("graph")

    @pl.when(i == 0)
    def _():
        grad_out = jnp.zeros((H, H), F32)
        at = 0
        for cot in cots:
            for j in range(cot.shape[0] // TILE):
                tile = cot[j * TILE : (j + 1) * TILE, :]
                cot_w[at] = dot(tile, w_out[...], 1, 1).astype(BF16)
                hi, lo = split(p_in[at])
                grad_out += dot(hi, tile, 0, 0) + dot(lo, tile, 0, 0)
                at += 1
        out[:H] = grad_out.astype(out.dtype)
        total[...] = jnp.zeros_like(total)

    parts = []
    for j in range(per):
        slot = dst[i * per + j, 0] ^ me
        grad_act = dot(pw[j], cot_w[slot], 0, 0)
        parts.append((grad_act * d_in[j * TILE : (j + 1) * TILE, :]).astype(BF16))
    grad_pre = jnp.concatenate(parts, axis=0)
    total[:H] += dot(grad_pre, jnp.concatenate([nodes[...], a_in[...]], axis=1), 0, 0)
    total[H:, :H] += jnp.sum(grad_pre.astype(F32).reshape(-1, 8, H), axis=0)

    @pl.when(i == pl.num_programs(0) - 1)
    def _():
        out[H : 2 * H] = total[:H, :H].astype(out.dtype)
        out[2 * H : 3 * H] = total[:H, H:].astype(out.dtype)
        row = jnp.sum(total[H:, :H], axis=0, keepdims=True)
        first = lax.broadcasted_iota(jnp.int32, (16, H), 0) == 0
        out[3 * H :] = jnp.where(first, row, 0.0).astype(out.dtype)


def finish_kernel(scale, mine, other, w_msg, w_in, g_msg, g_in, g_bias, g_out):
    sums = (mine[...].astype(F32) + other[...].astype(F32)) * scale
    g_out[...] = sums[:H]
    g_in[:H] = sums[H : 2 * H].T
    hi, lo = split(sums[2 * H : 3 * H])
    g_in[H:] = dot(w_msg[...], hi, 0, 1) + dot(w_msg[...], lo, 0, 1)
    w_low = w_in[H:]
    g_msg[...] = dot(hi, w_low, 0, 1) + dot(lo, w_low, 0, 1)
    g_bias[...] = sums[3 * H : 3 * H + 1]


def on_device(
    nodes, adjacency, tile_src, pool_dst, pool_weight, coarse_cot, w_msg, w_in, b_in, w_out
):
    feats = nodes[0]
    adj = adjacency[0]
    src = tile_src[0]
    dst = pool_dst[0]
    pw = pool_weight[0]
    cot = coarse_cot[0]
    rows = feats.shape[0]
    count = rows // TILE
    slabs = lax.axis_size("graph")
    designs = lax.axis_size("design")
    assert slabs & (slabs - 1) == 0 and designs & (designs - 1) == 0 and slabs > 1
    steps = STEPS
    assert count % steps == 0 and steps % 4 == 0
    per = count // steps
    block = per * TILE
    levels = slabs.bit_length()
    margin = HT * TILE
    bias = b_in.reshape(1, H)

    odd = lax.axis_index("graph") & 1
    first, last = feats[:margin], feats[rows - margin :]
    near_send = jnp.where(odd == 0, last, first)
    far_send = jnp.where(odd == 0, first, last)
    near_msg = exchange(jnp.concatenate([cot, near_send], axis=0), "graph", 1)
    across = [(i, i + 1) for i in range(1, slabs - 1, 2)]
    far = lax.ppermute(far_send, "graph", across + [(b, a) for a, b in across])
    near = near_msg[TILE:]
    cots = [cot, near_msg[:TILE]]
    for level in range(1, levels - 1):
        cots.append(exchange(jnp.concatenate(cots, axis=0), "graph", 1 << level))

    smem = pl.BlockSpec(memory_space=pltpu.SMEM)
    vmem = pl.BlockSpec(memory_space=pltpu.VMEM)
    hbm = pl.BlockSpec(memory_space=pl.ANY)
    acc_shape = (slabs, TILE, 2 * H)
    base = steps // 4
    params = pltpu.CompilerParams(
        dimension_semantics=("arbitrary",), vmem_limit_bytes=40 * 1024 * 1024
    )

    def tiles(where):
        return pl.BlockSpec((per, TILE, TILE), lambda i: (where(i), 0, 0))

    def edges(where):
        return pl.BlockSpec((per, NBR, TILE, TILE), lambda i: (where(i), 0, 0, 0))

    def row_block(where):
        return pl.BlockSpec((block, H), lambda i: (where(i), 0))

    inner = lambda i: i + base
    a_mid, d_mid, acc_mid = pl.pallas_call(
        lambda *refs: inner_kernel(per, base, *refs),
        grid=(steps // 2,),
        in_specs=[smem, smem, hbm, edges(inner), tiles(inner), vmem, vmem, vmem],
        out_specs=[row_block(inner), row_block(inner), vmem],
        out_shape=[
            jax.ShapeDtypeStruct((rows, H), BF16),
            jax.ShapeDtypeStruct((rows, H), F32),
            jax.ShapeDtypeStruct(acc_shape, F32),
        ],
        scratch_shapes=[
            pltpu.VMEM((rows + 2 * margin, H), BF16),
            pltpu.VMEM((2 * H, H), BF16),
            pltpu.SemaphoreType.DMA,
        ],
        compiler_params=params,
        cost_estimate=pl.CostEstimate(
            flops=8 * rows * H * H, bytes_accessed=rows * H * 9, transcendentals=rows * H // 2
        ),
        name="inner",
    )(src, dst, feats, adj, pw, w_msg, w_in, bias)

    order = bit_order(slabs)
    outer = lambda i: outer_block(i, steps)
    half = (slabs // 2, TILE, H)
    a_all, d_all, p_all, send, keep = pl.pallas_call(
        lambda *refs: outer_kernel(per, steps, order, *refs),
        grid=(steps // 2,),
        in_specs=[
            smem, smem, hbm, hbm, hbm, edges(outer), tiles(outer), vmem, vmem, vmem, vmem,
            vmem, hbm, hbm,
        ],
        out_specs=[row_block(outer), row_block(outer), vmem, vmem, vmem],
        out_shape=[
            jax.ShapeDtypeStruct((rows, H), BF16),
            jax.ShapeDtypeStruct((rows, H), F32),
            jax.ShapeDtypeStruct((slabs, TILE, H), F32),
            jax.ShapeDtypeStruct(half, BF16),
            jax.ShapeDtypeStruct(half, F32),
        ],
        scratch_shapes=[
            pltpu.VMEM((rows + 2 * margin, H), BF16),
            pltpu.VMEM((2 * H, H), BF16),
            pltpu.VMEM(acc_shape, F32),
            pltpu.SemaphoreType.DMA((3,)),
        ],
        input_output_aliases={12: 0, 13: 1},
        compiler_params=params,
        cost_estimate=pl.CostEstimate(
            flops=8 * rows * H * H, bytes_accessed=rows * H * 9, transcendentals=rows * H // 2
        ),
        name="outer",
    )(src, dst, feats, near, far, adj, pw, w_msg, w_in, bias, w_out, acc_mid, a_mid, d_mid)

    same = lambda i: i
    partial = pl.pallas_call(
        lambda *refs: backward_kernel(per, levels, *refs),
        grid=(steps,),
        in_specs=[smem] + [vmem] * levels
        + [row_block(same), row_block(same), row_block(same), tiles(same), vmem, vmem],
        out_specs=vmem,
        out_shape=jax.ShapeDtypeStruct((3 * H + 16, H), BF16),
        scratch_shapes=[
            pltpu.VMEM((slabs, TILE, H), BF16),
            pltpu.VMEM((H + 8, 2 * H), F32),
        ],
        compiler_params=params,
        cost_estimate=pl.CostEstimate(
            flops=6 * rows * H * H, bytes_accessed=rows * H * 10, transcendentals=0
        ),
        name="backward",
    )(dst, *cots, feats, a_all, d_all, pw, p_all, w_out)

    got = exchange(send, "graph", 1)
    held = keep + got.astype(F32)
    mask = 2
    while mask < slabs:
        size = held.shape[0] // 2
        got = exchange(held[size:].astype(BF16), "graph", mask)
        held = held[:size] + got.astype(F32)
        mask *= 2
    coarse = held[0].astype(BF16)

    rounds = [("design", 1 << b) for b in range(designs.bit_length() - 1)]
    rounds += [("graph", 1 << b) for b in range(slabs.bit_length() - 1)]
    mine = partial
    for axis, mask in rounds[:-1]:
        mine = (mine.astype(F32) + exchange(mine, axis, mask).astype(F32)).astype(BF16)
    other = exchange(mine, *rounds[-1])
    scale = 1.0 / math.sqrt(designs * rows * slabs)
    g_msg, g_in, g_bias, g_out = pl.pallas_call(
        lambda *refs: finish_kernel(scale, *refs),
        in_specs=[vmem] * 4,
        out_specs=[vmem] * 4,
        out_shape=[
            jax.ShapeDtypeStruct((H, H), F32),
            jax.ShapeDtypeStruct((2 * H, H), F32),
            jax.ShapeDtypeStruct((1, H), F32),
            jax.ShapeDtypeStruct((H, H), F32),
        ],
        name="finish",
    )(mine, other, w_msg, w_in)

    size = rows // steps

    def fine_kernel(nodes_ref, a_ref, w_msg_ref, w_in_ref, bias_ref, w_out_ref, out, wcat):
        @pl.when(pl.program_id(0) == 0)
        def _():
            join_weights(w_msg_ref, w_in_ref, wcat)

        own = nodes_ref[...]
        pre = dot(jnp.concatenate([own, a_ref[...]], axis=1), wcat[...]) + bias_ref[...]
        act = (pre * (0.5 * jnp.tanh(0.5 * pre) + 0.5)).astype(BF16)
        out[...] = (own.astype(F32) + dot(act, w_out_ref[...])).astype(BF16)

    fine = pl.pallas_call(
        fine_kernel,
        grid=(steps,),
        in_specs=[row_block(same), row_block(same), vmem, vmem, vmem, vmem],
        out_specs=row_block(same),
        out_shape=jax.ShapeDtypeStruct((rows, H), BF16),
        scratch_shapes=[pltpu.VMEM((2 * H, H), BF16)],
        compiler_params=params,
        cost_estimate=pl.CostEstimate(
            flops=6 * rows * H * H, bytes_accessed=rows * H * 6, transcendentals=rows * H
        ),
        name="fine",
    )(feats, a_all, w_msg, w_in, bias, w_out)
    return fine[None], coarse[None], g_msg, g_in, g_bias.reshape(H), g_out


def solution(mesh):
    in_specs = (
        P("design", "graph", None),
        P("design", "graph", None, None, None),
        P("design", "graph", None),
        P("design", "graph", None),
        P("design", "graph", None, None),
        P("design", "graph", None),
        P(),
        P(),
        P(),
        P(),
    )
    out_specs = (P("design", "graph", None), P("design", "graph", None), P(), P(), P(), P())
    return jax.shard_map(
        on_device, mesh=mesh, in_specs=in_specs, out_specs=out_specs, check_vma=False
    )
```

```python
import math

import jax
import jax.numpy as jnp
from jax import lax
from jax.experimental import pallas as pl
from jax.experimental.pallas import tpu as pltpu
from jax.sharding import PartitionSpec as P

H = 128
TILE = 128
NBR = 4
HT = 2
QUAD = 4
BODY = 4
F32 = jnp.float32
BF16 = jnp.bfloat16
MARGIN = HT * TILE
HALF = H // 2
PACK = 3 * HALF


def dot(a, b, ca=1, cb=0):
    return lax.dot_general(a, b, (((ca,), (cb,)), ((), ())), preferred_element_type=F32)


def split(x):
    hi = x.astype(BF16)
    return hi, (x - hi.astype(F32)).astype(BF16)


def diagonal(a, b):
    top = jnp.concatenate([a, jnp.zeros(b.shape, b.dtype)], axis=1)
    low = jnp.concatenate([jnp.zeros(a.shape, a.dtype), b], axis=1)
    return jnp.concatenate([top, low], axis=0)


def beside(a, b):
    return jnp.concatenate([a, b], axis=1)


def bit_order(count):
    bits = count.bit_length() - 1
    return [sum(((q >> b) & 1) << (bits - 1 - b) for b in range(bits)) for q in range(count)]


def exchange(x, axis, mask):
    return lax.ppermute(x, axis, [(i, i ^ mask) for i in range(lax.axis_size(axis))])


def rows_at(tile, count=1):
    return pl.ds(pl.multiple_of(tile * TILE, TILE), count * TILE)


def pack_kernel(nodes, near, far, sem):
    odd = lax.axis_index("graph") & 1
    gap = nodes.shape[0] - MARGIN
    near_at = pl.multiple_of((1 - odd) * gap, TILE)
    far_at = pl.multiple_of(odd * gap, TILE)
    copies = [
        pltpu.make_async_copy(nodes.at[pl.ds(near_at, MARGIN)], near, sem.at[0]),
        pltpu.make_async_copy(nodes.at[pl.ds(far_at, MARGIN)], far, sem.at[1]),
    ]
    for copy in copies:
        copy.start()
    for copy in copies:
        copy.wait()


def join_weights(w_msg, w_in, wcat):
    wcat[:H] = (0.5 * w_in[:H].astype(F32)).astype(BF16)
    wcat[H:] = (0.5 * dot(w_msg[...], w_in[H:])).astype(BF16)


def spans(count):
    quads = count // QUAD
    low = quads // 2 - quads // 8
    middle = list(range(low, low + quads // 4))
    return middle, [q for q in range(quads) if q not in middle]


def run_stages(count, *stages):
    held = {}
    for tick in range(count + len(stages) - 1):
        for k, stage in enumerate(stages):
            i = tick - k
            if 0 <= i < count:
                held[k, i] = stage(i, held.get((k - 1, i)))


def forward_quads(firsts, at_adj, src, dst, ext, adj, pw, wcat, bias, outs, acc, ready=None):
    a_out, act_out, slope_out = outs
    me = lax.axis_index("graph")
    h_bias = 0.5 * bias[...]

    def gather(i, _):
        if ready is not None:
            ready(i)
        sums = []
        for j in range(QUAD):
            t = firsts[i] + j
            picked = [ext[rows_at(src[k, t]), :] for k in range(NBR)]
            weights = jnp.concatenate([adj[at_adj[i] + j, k] for k in range(NBR)], axis=1)
            sums.append(dot(weights, jnp.concatenate(picked, axis=0)).astype(BF16))
        summed = jnp.concatenate(sums, axis=0)
        a_out[rows_at(firsts[i], QUAD), :] = summed
        return summed

    def activate(i, summed):
        own = ext[rows_at(firsts[i] + HT, QUAD), :]
        h = dot(beside(own, summed), wcat[...]) + h_bias
        s = jnp.tanh(h)
        hs = h * s
        act = (h + hs).astype(BF16)
        act_out[rows_at(firsts[i], QUAD), :] = act
        slope = (1.0 + s) * ((1.0 + h) - hs)
        for j in range(QUAD):
            slope_out[firsts[i] + j] = slope[j * TILE : (j + 1) * TILE].T
        return act

    def pool(i, act):
        add_pooled(firsts[i], act, dst, me, pw, acc)

    run_stages(len(firsts), gather, activate, pool)


def add_pooled(first, values, dst, me, pw, acc):
    for j in range(0, QUAD, 2):
        a, b = values[j * TILE : (j + 1) * TILE], values[(j + 1) * TILE : (j + 2) * TILE]
        t = first + j
        term = dot(beside(pw[t], pw[t + 1]), diagonal(a, b))
        acc[dst[0, t] ^ me] += term[:, :H]
        acc[dst[0, t + 1] ^ me] += term[:, H:]


def inner_kernel(
    middle, rest, src, dst, nodes, adj, pw, w_msg, w_in, bias,
    ext, adj_v, pw_v, a_out, act_out, slope_out, acc, wcat, adj_m, sem,
):
    quads = len(middle) + len(rest)
    chunk = QUAD * TILE
    near = [middle[0] - 1] + middle + [middle[-1] + 1]
    far = [q for q in range(quads) if q not in near]

    def node_copy(q):
        return pltpu.make_async_copy(
            nodes.at[pl.ds(q * chunk, chunk)],
            ext.at[pl.ds(MARGIN + q * chunk, chunk)],
            sem.at[0, q],
        )

    def pool_copy(q):
        part = pl.ds(q * QUAD, QUAD)
        return pltpu.make_async_copy(pw.at[part], pw_v.at[part], sem.at[1, q])

    def edge_copy(q):
        to, n = (adj_m, middle.index(q)) if q in middle else (adj_v, rest.index(q))
        return pltpu.make_async_copy(
            adj.at[pl.ds(q * QUAD, QUAD)], to.at[pl.ds(n * QUAD, QUAD)], sem.at[2, q]
        )

    first = [edge_copy(middle[0])] + [node_copy(q) for q in near]
    first += [edge_copy(q) for q in middle[1:]] + [pool_copy(q) for q in middle]
    later = [node_copy(q) for q in far] + [edge_copy(q) for q in rest]
    later += [pool_copy(q) for q in rest]
    for copy in first + later:
        copy.start()
    join_weights(w_msg, w_in, wcat)
    acc[...] = jnp.zeros_like(acc)

    def ready(i):
        if i == 0:
            for q in near[:3]:
                node_copy(q).wait()
        elif near[i + 2 :]:
            node_copy(near[i + 2]).wait()
        edge_copy(middle[i]).wait()
        pool_copy(middle[i]).wait()

    forward_quads(
        [q * QUAD for q in middle], [n * QUAD for n in range(len(middle))], src, dst, ext,
        adj_m, pw_v, wcat, bias, (a_out, act_out, slope_out), acc, ready,
    )
    for copy in later:
        copy.wait()


def outer_kernel(
    middle, rest, src, dst, near, far, w_msg, w_in, bias,
    ext_in, a_in, act_in, slope_in, acc_in, adj, pw,
    ext, a_out, act_out, slope_out, p_out, acc, wcat,
):
    odd = lax.axis_index("graph") & 1
    right = ext.shape[0] - MARGIN
    ext[pl.ds(pl.multiple_of((1 - odd) * right, TILE), MARGIN), :] = near[...]
    ext[pl.ds(pl.multiple_of(odd * right, TILE), MARGIN), :] = far[...]
    join_weights(w_msg, w_in, wcat)
    acc[...] = acc_in[...]

    def body(step, _):
        spots = [step * BODY + n for n in range(BODY)]
        firsts = [QUAD * jnp.where(s < middle[0], s, s + len(middle)) for s in spots]
        forward_quads(
            firsts, [QUAD * s for s in spots], src, dst, ext, adj, pw, wcat, bias,
            (a_out, act_out, slope_out), acc,
        )
        return 0

    lax.fori_loop(0, len(rest) // BODY, body, 0)
    for r in range(acc.shape[0]):
        hi, lo = split(acc[r])
        p_out[r * TILE : (r + 1) * TILE, :H] = hi
        p_out[r * TILE : (r + 1) * TILE, H:] = lo


def backward_kernel(pieces, dst, *refs):
    cots = refs[:pieces]
    (ext, a_in, slope_in, pw, p_in, w_out) = refs[pieces : pieces + 6]
    keep, send, cot_all, cot_w, total, bias, mats = refs[pieces + 6 :]
    me = lax.axis_index("graph")
    core = lax.axis_index("design") & 1
    at = 0
    for cot in cots:
        size = cot.shape[0]
        cot_all[at : at + size] = cot[...]
        at += size
    for r in range(cot_w.shape[0]):
        tile = cot_all[r * TILE : (r + 1) * TILE]
        cot_w[r] = (0.5 * dot(w_out[...], tile, 1, 1)).astype(BF16)
    both = dot(cot_all[...], p_in[...], 0, 0)
    mats[0] = both[:, :H] + both[:, H:]
    total[...] = jnp.zeros_like(total)
    bias[...] = jnp.zeros_like(bias)

    def body(step, _):
        firsts = [(step * BODY + n) * QUAD for n in range(BODY)]

        def unpool(i, _):
            parts = []
            for j in range(0, QUAD, 2):
                t = firsts[i] + j
                left = beside(cot_w[dst[0, t] ^ me], cot_w[dst[0, t + 1] ^ me])
                parts.append(dot(left, diagonal(pw[t], pw[t + 1])))
            return parts

        def slopes(i, parts):
            done = []
            for j, part in enumerate(parts):
                t = firsts[i] + 2 * j
                grad = part * beside(slope_in[t], slope_in[t + 1])
                bias[...] += grad
                done.append(grad.astype(BF16))
            return jnp.concatenate(done, axis=1)

        def weights(i, grad_pre):
            own = ext[rows_at(firsts[i] + HT, QUAD), :]
            total[...] += dot(grad_pre, beside(own, a_in[rows_at(firsts[i], QUAD), :]))

        run_stages(BODY, unpool, slopes, weights)
        return 0

    lax.fori_loop(0, slope_in.shape[0] // (QUAD * BODY), body, 0)
    mats[1] = total[:, :H]
    mats[2] = total[:, H:]
    column = jnp.sum(bias[...], axis=1, keepdims=True)
    row = jnp.broadcast_to(column, (H, H)).T[:8]
    for out, half in ((keep, core), (send, 1 - core)):
        for m in range(3):
            at = pl.multiple_of(half * HALF, HALF)
            out[m * HALF : (m + 1) * HALF] = mats[m, pl.ds(at, HALF), :]
        out[PACK:] = row


def tail_kernel(order, dst, ext, act_in, pw, w_out, fine, send, keep, acc, wdiag, out_v, sem):
    me = lax.axis_index("graph")
    wdiag[...] = diagonal(w_out[...], w_out[...])
    acc[...] = jnp.zeros_like(acc)
    chunk = QUAD * BODY
    steps = act_in.shape[0] // (chunk * TILE)
    half = QUAD * TILE // 2

    def copy(step):
        part = rows_at(step * chunk, chunk)
        return pltpu.make_async_copy(out_v.at[part], fine.at[part], sem.at[step])

    def body(step, _):
        firsts = [(step * BODY + n) * QUAD for n in range(BODY)]

        def project(i, _):
            act = act_in[rows_at(firsts[i], QUAD), :]
            return dot(beside(act[:half], act[half:]), wdiag[...])

        def update(i, delta):
            own = ext[rows_at(firsts[i] + HT, QUAD), :].astype(F32)
            out = jnp.concatenate([own[:half] + delta[:, :H], own[half:] + delta[:, H:]], axis=0)
            out = out.astype(BF16)
            out_v[rows_at(firsts[i], QUAD), :] = out
            return out

        def pool(i, out):
            add_pooled(firsts[i], out, dst, me, pw, acc)

        run_stages(BODY, project, update, pool)
        copy(step).start()
        return 0

    lax.fori_loop(0, steps, body, 0)
    count = len(order)
    for q, r in enumerate(order):
        if q < count // 2:
            keep[q] = acc[r]
        else:
            send[q - count // 2] = acc[r].astype(BF16)

    def drain(step, _):
        copy(step).wait()
        return 0

    lax.fori_loop(0, steps, drain, 0)


def finish_kernel(scale, held, other, w_msg, w_in, g_msg, g_in, g_bias, g_out, mats):
    core = lax.axis_index("design") & 1
    for part, half in ((held, core), (other, 1 - core)):
        for m in range(3):
            at = pl.multiple_of(half * HALF, HALF)
            mats[m, pl.ds(at, HALF), :] = part[m * HALF : (m + 1) * HALF] * scale
    g_out[...] = mats[0].T
    g_in[:H] = mats[1].T
    hi, lo = split(mats[2])
    g_in[H:] = dot(w_msg[...], hi, 0, 1) + dot(w_msg[...], lo, 0, 1)
    w_low = w_in[H:]
    g_msg[...] = dot(hi, w_low, 0, 1) + dot(lo, w_low, 0, 1)
    g_bias[...] = jnp.where(core == 0, held[PACK : PACK + 1], other[PACK : PACK + 1]) * scale


def on_device(
    nodes, adjacency, tile_src, pool_dst, pool_weight, coarse_cot, w_msg, w_in, b_in, w_out
):
    def stay(x):
        return pltpu.with_memory_space_constraint(x, pltpu.HBM)

    feats = stay(nodes[0])
    adj = stay(adjacency[0])
    src = tile_src[0].T
    dst = pool_dst[0].T
    pw = stay(pool_weight[0])
    cot = coarse_cot[0]
    rows = feats.shape[0]
    count = rows // TILE
    slabs = lax.axis_size("graph")
    designs = lax.axis_size("design")
    assert slabs & (slabs - 1) == 0 and designs & (designs - 1) == 0
    assert slabs > 1 and designs > 1
    assert count % (4 * QUAD * BODY) == 0
    middle, rest = spans(count)
    bias = stay(b_in.reshape(1, H))
    w_msg, w_in, w_out = stay(w_msg), stay(w_in), stay(w_out)

    smem = pl.BlockSpec(memory_space=pltpu.SMEM)
    vmem = pl.BlockSpec(memory_space=pltpu.VMEM)
    hbm = pl.BlockSpec(memory_space=pl.ANY)

    def shape(*dims, dtype=F32):
        return jax.ShapeDtypeStruct(dims, dtype)

    def fixed(x):
        return pl.BlockSpec(x.shape, lambda *_: (0,) * x.ndim)

    def params(mib):
        return pltpu.CompilerParams(vmem_limit_bytes=mib * 1024 * 1024)

    def cost(units, mib, trans=0):
        return pl.CostEstimate(
            flops=2 * units * rows * H * H,
            bytes_accessed=mib * 1024 * 1024,
            transcendentals=trans,
        )

    first = [m for m in (1, 2, 3) if m < slabs] + [1 << b for b in range(2, slabs.bit_length() - 1)]
    cots = {0: cot}
    for mask in first:
        cots[mask] = exchange(cot, "graph", mask)

    near_send, far_send = pl.pallas_call(
        pack_kernel,
        in_specs=[hbm],
        out_specs=[vmem, vmem],
        out_shape=[shape(MARGIN, H, dtype=BF16)] * 2,
        scratch_shapes=[pltpu.SemaphoreType.DMA((2,))],
        compiler_params=params(1),
        name="pack",
    )(feats)
    near = exchange(near_send, "graph", 1)
    across = [(i, i + 1) for i in range(1, slabs - 1, 2)]
    far = lax.ppermute(far_send, "graph", across + [(b, a) for a, b in across])

    ext_shape = shape(rows + 2 * MARGIN, H, dtype=BF16)
    row_shape = shape(rows, H, dtype=BF16)
    slope_shape = shape(count, H, TILE)
    acc_shape = shape(slabs, TILE, H)
    adj_shape = shape(len(rest) * QUAD, NBR, TILE, TILE, dtype=BF16)
    wcat = pltpu.VMEM((2 * H, H), BF16)

    ext, adj_v, pw_v, a_mid, act_mid, slope_mid, acc_mid = pl.pallas_call(
        lambda *refs: inner_kernel(middle, rest, *refs),
        in_specs=[smem, smem, hbm, hbm, hbm, fixed(w_msg), fixed(w_in), fixed(bias)],
        out_specs=[vmem] * 7,
        out_shape=[
            ext_shape, adj_shape, shape(*pw.shape, dtype=BF16), row_shape, row_shape,
            slope_shape, acc_shape,
        ],
        scratch_shapes=[
            wcat,
            pltpu.VMEM((len(middle) * QUAD, NBR, TILE, TILE), BF16),
            pltpu.SemaphoreType.DMA((3, count // QUAD)),
        ],
        compiler_params=params(12),
        cost_estimate=cost(2, 12, rows * H // 4),
        name="inner",
    )(src, dst, feats, adj, pw, w_msg, w_in, bias)

    ext, a_all, act_all, slope_all, p_all = pl.pallas_call(
        lambda *refs: outer_kernel(middle, rest, *refs),
        in_specs=[smem, smem, vmem, vmem, fixed(w_msg), fixed(w_in), fixed(bias)] + [vmem] * 7,
        out_specs=[vmem] * 5,
        out_shape=[
            ext_shape, row_shape, row_shape, slope_shape,
            shape(slabs * TILE, 2 * H, dtype=BF16),
        ],
        scratch_shapes=[pltpu.VMEM((slabs, TILE, H), F32), wcat],
        input_output_aliases={7: 0, 8: 1, 9: 2, 10: 3},
        compiler_params=params(12),
        cost_estimate=cost(6, 8, rows * H // 2),
        name="outer",
    )(
        src, dst, near, far, w_msg, w_in, bias, ext, a_mid, act_mid, slope_mid, acc_mid,
        adj_v, pw_v,
    )

    for b in range(2, slabs.bit_length() - 1):
        mask = 1 << b
        known = list(range(1, mask))
        got = exchange(jnp.concatenate([cots[r] for r in known], axis=0), "graph", mask)
        for n, r in enumerate(known):
            cots[mask + r] = got[n * TILE : (n + 1) * TILE]

    every = [cots[r] for r in range(slabs)]
    keep, send = pl.pallas_call(
        lambda *refs: backward_kernel(len(every), *refs),
        in_specs=[smem]
        + [vmem] * len(every)
        + [vmem] * 5
        + [fixed(w_out)],
        out_specs=[vmem, vmem],
        out_shape=[shape(PACK + 8, H)] * 2,
        scratch_shapes=[
            pltpu.VMEM((slabs * TILE, H), BF16),
            pltpu.VMEM((slabs, H, TILE), BF16),
            pltpu.VMEM((H, 2 * H), F32),
            pltpu.VMEM((H, 2 * H), F32),
            pltpu.VMEM((3, H, H), F32),
        ],
        compiler_params=params(16),
        cost_estimate=cost(3, 4),
        name="backward",
    )(dst, *every, ext, a_all, slope_all, pw_v, p_all, w_out)

    order = bit_order(slabs)
    fine, c_send, c_keep = pl.pallas_call(
        lambda *refs: tail_kernel(order, *refs),
        in_specs=[smem, vmem, vmem, vmem, fixed(w_out)],
        out_specs=[hbm, vmem, vmem],
        out_shape=[
            row_shape,
            shape(slabs // 2, TILE, H, dtype=BF16),
            shape(slabs // 2, TILE, H),
        ],
        scratch_shapes=[
            pltpu.VMEM((slabs, TILE, H), F32),
            pltpu.VMEM((2 * H, 2 * H), BF16),
            pltpu.VMEM((rows, H), BF16),
            pltpu.SemaphoreType.DMA((count // (QUAD * BODY),)),
        ],
        compiler_params=params(16),
        cost_estimate=cost(2, 4),
        name="tail",
    )(dst, ext, act_all, pw_v, w_out)

    held = c_keep + exchange(c_send, "graph", 1).astype(F32)
    mask = 2
    while mask < slabs:
        size = held.shape[0] // 2
        got = exchange(held[size:].astype(BF16), "graph", mask)
        held = held[:size] + got.astype(F32)
        mask *= 2
    coarse = held[0].astype(BF16)

    rounds = [("design", 1 << b) for b in range(1, designs.bit_length() - 1)]
    rounds += [("graph", 1 << b) for b in range(slabs.bit_length() - 1)]
    mine = keep + exchange(send, "design", 1)
    for axis, mask in rounds:
        mine = mine + exchange(mine, axis, mask)
    other = exchange(mine, "design", 1)
    scale = 1.0 / math.sqrt(designs * rows * slabs)
    g_msg, g_in, g_bias, g_out = pl.pallas_call(
        lambda *refs: finish_kernel(scale, *refs),
        in_specs=[vmem, vmem, fixed(w_msg), fixed(w_in)],
        out_specs=[vmem] * 4,
        out_shape=[shape(H, H), shape(2 * H, H), shape(1, H), shape(H, H)],
        scratch_shapes=[pltpu.VMEM((3, H, H), F32)],
        compiler_params=params(4),
        name="finish",
    )(mine, other, w_msg, w_in)
    return fine[None], coarse[None], g_msg, g_in, g_bias.reshape(H), g_out


def solution(mesh):
    in_specs = (
        P("design", "graph", None),
        P("design", "graph", None, None, None),
        P("design", "graph", None),
        P("design", "graph", None),
        P("design", "graph", None, None),
        P("design", "graph", None),
        P(),
        P(),
        P(),
        P(),
    )
    out_specs = (P("design", "graph", None), P("design", "graph", None), P(), P(), P(), P())
    return jax.shard_map(
        on_device, mesh=mesh, in_specs=in_specs, out_specs=out_specs, check_vma=False
    )
```

```python
import math

import jax
import jax.numpy as jnp
from jax import lax
from jax.experimental import pallas as pl
from jax.experimental.pallas import tpu as pltpu
from jax.sharding import PartitionSpec as P


H = 128
TILE = 128
NBR = 4
HT = 2
QUAD = 4
F32 = jnp.float32
BF16 = jnp.bfloat16
MARGIN = HT * TILE
HALF = H // 2
PACK = 3 * HALF
LOW_ROUNDS = 1


def dot(a, b, ca=1, cb=0):
    return lax.dot_general(a, b, (((ca,), (cb,)), ((), ())), preferred_element_type=F32)


def split(x):
    hi = x.astype(BF16)
    return hi, (x - hi.astype(F32)).astype(BF16)


def diagonal(a, b):
    top = jnp.concatenate([a, jnp.zeros(b.shape, b.dtype)], axis=1)
    low = jnp.concatenate([jnp.zeros(a.shape, a.dtype), b], axis=1)
    return jnp.concatenate([top, low], axis=0)


def beside(a, b):
    return jnp.concatenate([a, b], axis=1)


def bit_order(count):
    bits = count.bit_length() - 1
    return [sum(((q >> b) & 1) << (bits - 1 - b) for b in range(bits)) for q in range(count)]


def exchange(x, axis, mask):
    return lax.ppermute(x, axis, [(i, i ^ mask) for i in range(lax.axis_size(axis))])


def rows_at(tile, count=1):
    if isinstance(tile, int):
        return pl.ds(tile * TILE, count * TILE)
    return pl.ds(pl.multiple_of(tile * TILE, TILE), count * TILE)


def pack_kernel(nodes, cot, near, far, sem):
    odd = lax.axis_index("graph") & 1
    gap = nodes.shape[0] - MARGIN
    near_at = pl.multiple_of((1 - odd) * gap, TILE)
    far_at = pl.multiple_of(odd * gap, TILE)
    copies = [
        pltpu.make_async_copy(cot, near.at[pl.ds(0, TILE)], sem.at[0]),
        pltpu.make_async_copy(
            nodes.at[pl.ds(near_at, MARGIN)], near.at[pl.ds(TILE, MARGIN)], sem.at[1]
        ),
        pltpu.make_async_copy(nodes.at[pl.ds(far_at, MARGIN)], far, sem.at[2]),
    ]
    for copy in copies:
        copy.start()
    for copy in copies:
        copy.wait()


def join_weights(w_msg, w_in, wcat):
    wcat[:H] = (0.5 * w_in[:H].astype(F32)).astype(BF16)
    wcat[H:] = (0.5 * dot(w_msg[...], w_in[H:])).astype(BF16)


def shares(quads):
    order = sorted(range(quads), key=lambda q: abs(2 * q - quads + 1))
    one, two = quads * 3 // 8, quads * 6 // 8
    return sorted(order[:one]), sorted(order[one:two]), sorted(order[two:])


def run_stages(count, *stages):
    held = {}
    for tick in range(count + len(stages) - 1):
        for k, stage in enumerate(stages):
            i = tick - k
            if 0 <= i < count:
                held[k, i] = stage(i, held.get((k - 1, i)))


def forward_quads(quads, src, dst, nodes, adj, pw, wcat, bias, outs, acc, edges=None):
    a_out, act_out, slope_out = outs
    me = lax.axis_index("graph")
    h_bias = 0.5 * bias[...]
    total = slope_out.shape[0]
    ends = {0: 0, total // QUAD - 1: 2 * (QUAD + 2 * HT) - total - 2 * HT}

    def gather(i, _):
        sums = []
        for j in range(QUAD):
            t = quads[i] * QUAD + j
            held, shift = (edges, ends[quads[i]]) if quads[i] in ends else (nodes, -HT)
            picked = [held[rows_at(src[k, t] + shift), :] for k in range(NBR)]
            weights = jnp.concatenate([adj[t, k] for k in range(NBR)], axis=1)
            sums.append(dot(weights, jnp.concatenate(picked, axis=0)).astype(BF16))
        summed = jnp.concatenate(sums, axis=0)
        a_out[rows_at(quads[i] * QUAD, QUAD), :] = summed
        return summed

    def activate(i, summed):
        first = quads[i] * QUAD
        own = nodes[rows_at(first, QUAD), :]
        h = dot(beside(own, summed), wcat[...]) + h_bias
        s = jnp.tanh(h)
        hs = h * s
        act = (h + hs).astype(BF16)
        act_out[rows_at(first, QUAD), :] = act
        slope = (1.0 + s) * ((1.0 + h) - hs)
        for j in range(QUAD):
            slope_out[first + j] = slope[j * TILE : (j + 1) * TILE].T
        return act

    def pool(i, act):
        add_pooled(quads[i] * QUAD, act, dst, me, pw, acc)

    run_stages(len(quads), gather, activate, pool)


def add_pooled(first, values, dst, me, pw, acc):
    for j in range(0, QUAD, 2):
        a, b = values[j * TILE : (j + 1) * TILE], values[(j + 1) * TILE : (j + 2) * TILE]
        t = first + j
        term = dot(beside(pw[t], pw[t + 1]), diagonal(a, b))
        acc[dst[0, t] ^ me] += term[:, :H]
        acc[dst[0, t + 1] ^ me] += term[:, H:]


def start_kernel(
    quads, src, dst, nodes, adj, pw, w_msg, w_in, bias, a_out, act_out, slope_out, acc, wcat
):
    join_weights(w_msg, w_in, wcat)
    acc[...] = jnp.zeros_like(acc)
    outs = (a_out, act_out, slope_out)
    forward_quads(quads, src, dst, nodes, adj, pw, wcat, bias, outs, acc)


def middle_kernel(
    quads, src, dst, nodes, adj, pw, wcat, bias, a_in, act_in, slope_in, acc_in,
    a_out, act_out, slope_out, acc,
):
    outs = (a_out, act_out, slope_out)
    forward_quads(quads, src, dst, nodes, adj, pw, wcat, bias, outs, acc)


def last_kernel(
    quads, order, src, dst, near, far, nodes, adj, pw, wcat, bias, w_out,
    a_in, act_in, slope_in, acc_in,
    a_out, act_out, slope_out, p_out, fine, send, keep,
    acc, pooled, edges, wdiag, out_v, sem,
):
    me = lax.axis_index("graph")
    odd = me & 1
    size = edges.shape[0]
    span = size // 2 - MARGIN
    edges[MARGIN : MARGIN + span] = nodes[:span]
    edges[size - MARGIN - span : size - MARGIN] = nodes[nodes.shape[0] - span :]
    edges[pl.ds(pl.multiple_of((1 - odd) * (size - MARGIN), TILE), MARGIN), :] = near[TILE:]
    edges[pl.ds(pl.multiple_of(odd * (size - MARGIN), TILE), MARGIN), :] = far[...]
    wdiag[...] = diagonal(w_out[...], w_out[...])
    acc[...] = acc_in[...]
    pooled[...] = jnp.zeros_like(pooled)
    outs = (a_out, act_out, slope_out)
    forward_quads(quads, src, dst, nodes, adj, pw, wcat, bias, outs, acc, edges)
    for r in range(acc.shape[0]):
        hi, lo = split(acc[r])
        p_out[r * TILE : (r + 1) * TILE, :H] = hi
        p_out[r * TILE : (r + 1) * TILE, H:] = lo

    half = QUAD * TILE // 2
    count = nodes.shape[0] // (QUAD * TILE)
    copies = []

    def project(i, _):
        act = act_out[rows_at(i * QUAD, QUAD), :]
        return dot(beside(act[:half], act[half:]), wdiag[...])

    def update(i, delta):
        part = rows_at(i * QUAD, QUAD)
        own = nodes[part, :].astype(F32)
        out = jnp.concatenate([own[:half] + delta[:, :H], own[half:] + delta[:, H:]], axis=0)
        out = out.astype(BF16)
        out_v[part, :] = out
        copies.append(pltpu.make_async_copy(out_v.at[part], fine.at[part], sem.at[i]))
        copies[-1].start()
        return out

    def pool(i, out):
        add_pooled(i * QUAD, out, dst, me, pw, pooled)

    run_stages(count, project, update, pool)
    slabs = len(order)
    for q, r in enumerate(order):
        if q < slabs // 2:
            keep[q] = pooled[r]
        else:
            send[q - slabs // 2] = pooled[r].astype(BF16)
    for copy in copies:
        copy.wait()


def backward_kernel(pieces, dst, *refs):
    cots = refs[:pieces]
    (nodes, a_in, slope_in, pw, p_in, w_out) = refs[pieces : pieces + 6]
    keep, send, cot_all, cot_w, total, bias, mats = refs[pieces + 6 :]
    me = lax.axis_index("graph")
    core = lax.axis_index("design") & 1
    at = 0
    for cot in cots:
        size = cot.shape[0]
        cot_all[at : at + size] = cot[...]
        at += size
    for r in range(cot_w.shape[0]):
        tile = cot_all[r * TILE : (r + 1) * TILE]
        cot_w[r] = (0.5 * dot(w_out[...], tile, 1, 1)).astype(BF16)
    both = dot(cot_all[...], p_in[...], 0, 0)
    mats[0] = both[:, :H] + both[:, H:]
    total[...] = jnp.zeros_like(total)
    bias[...] = jnp.zeros_like(bias)

    firsts = list(range(0, slope_in.shape[0], QUAD))

    def unpool(i, _):
        parts = []
        for j in range(0, QUAD, 2):
            t = firsts[i] + j
            left = beside(cot_w[dst[0, t] ^ me], cot_w[dst[0, t + 1] ^ me])
            parts.append(dot(left, diagonal(pw[t], pw[t + 1])))
        return parts

    def slopes(i, parts):
        done = []
        for j, part in enumerate(parts):
            t = firsts[i] + 2 * j
            grad = part * beside(slope_in[t], slope_in[t + 1])
            bias[...] += grad
            done.append(grad.astype(BF16))
        return jnp.concatenate(done, axis=1)

    def weights(i, grad_pre):
        own = nodes[rows_at(firsts[i], QUAD), :]
        total[...] += dot(grad_pre, beside(own, a_in[rows_at(firsts[i], QUAD), :]))

    run_stages(len(firsts), unpool, slopes, weights)

    mats[1] = total[:, :H]
    mats[2] = total[:, H:]
    column = jnp.sum(bias[...], axis=1, keepdims=True)
    row = jnp.broadcast_to(column, (H, H)).T[:8]
    for out, half in ((keep, core), (send, 1 - core)):
        for m in range(3):
            at = pl.multiple_of(half * HALF, HALF)
            out[m * HALF : (m + 1) * HALF] = mats[m, pl.ds(at, HALF), :]
        out[PACK:] = row


def finish_kernel(scale, held, other, w_msg, w_in, g_msg, g_in, g_bias, g_out, mats):
    core = lax.axis_index("design") & 1
    for part, half in ((held, core), (other, 1 - core)):
        for m in range(3):
            at = pl.multiple_of(half * HALF, HALF)
            mats[m, pl.ds(at, HALF), :] = part[m * HALF : (m + 1) * HALF] * scale
    g_out[...] = mats[0].T
    g_in[:H] = mats[1].T
    hi, lo = split(mats[2])
    g_in[H:] = dot(w_msg[...], hi, 0, 1) + dot(w_msg[...], lo, 0, 1)
    w_low = w_in[H:]
    g_msg[...] = dot(hi, w_low, 0, 1) + dot(lo, w_low, 0, 1)
    g_bias[...] = jnp.where(core == 0, held[PACK : PACK + 1], other[PACK : PACK + 1]) * scale


def layer(
    nodes, adjacency, tile_src, pool_dst, pool_weight, coarse_cot, w_msg, w_in, b_in, w_out
):
    def stay(x):
        return pltpu.with_memory_space_constraint(x, pltpu.HBM)

    feats = nodes[0]
    adj = adjacency[0]
    src = tile_src[0].T
    dst = pool_dst[0].T
    pw = pool_weight[0]
    cot = coarse_cot[0]
    rows = feats.shape[0]
    count = rows // TILE
    slabs = lax.axis_size("graph")
    designs = lax.axis_size("design")
    assert slabs & (slabs - 1) == 0 and designs & (designs - 1) == 0
    assert slabs > 1 and designs > 1
    assert count % (8 * QUAD) == 0
    one, two, three = shares(count // QUAD)
    bias = b_in.reshape(1, H)

    smem = pl.BlockSpec(memory_space=pltpu.SMEM)
    vmem = pl.BlockSpec(memory_space=pltpu.VMEM)
    hbm = pl.BlockSpec(memory_space=pl.ANY)

    def shape(*dims, dtype=F32):
        return jax.ShapeDtypeStruct(dims, dtype)

    def params(mib):
        return pltpu.CompilerParams(vmem_limit_bytes=mib * 1024 * 1024)

    def cost(units, mib, trans=0):
        return pl.CostEstimate(
            flops=2 * units * rows * H * H,
            bytes_accessed=mib * 1024 * 1024,
            transcendentals=trans,
        )

    near_send, far_send = pl.pallas_call(
        pack_kernel,
        in_specs=[hbm, hbm],
        out_specs=[vmem, vmem],
        out_shape=[shape(TILE + MARGIN, H, dtype=BF16), shape(MARGIN, H, dtype=BF16)],
        scratch_shapes=[pltpu.SemaphoreType.DMA((3,))],
        compiler_params=params(1),
        cost_estimate=cost(40, 40),
        name="pack",
    )(stay(feats), stay(cot))
    near = exchange(near_send, "graph", 1)
    across = [(i, i + 1) for i in range(1, slabs - 1, 2)]
    far = lax.ppermute(far_send, "graph", across + [(b, a) for a, b in across])

    row_shape = shape(rows, H, dtype=BF16)
    slope_shape = shape(count, H, TILE)
    acc_shape = shape(slabs, TILE, H)
    wcat_shape = shape(2 * H, H, dtype=BF16)
    state = [row_shape, row_shape, slope_shape]

    *held, wcat = pl.pallas_call(
        lambda *refs: start_kernel(one, *refs),
        in_specs=[smem, smem, vmem, vmem, vmem, vmem, vmem, vmem],
        out_specs=[vmem] * 5,
        out_shape=[*state, acc_shape, wcat_shape],
        compiler_params=params(8),
        cost_estimate=cost(3, 8, rows * H * 3 // 8),
        name="start",
    )(src, dst, feats, adj, pw, w_msg, w_in, bias)

    cots = [near_send[:TILE], near[:TILE]]
    pair = exchange(jnp.concatenate(cots, axis=0), "graph", 2) if slabs > 2 else None

    held = pl.pallas_call(
        lambda *refs: middle_kernel(two, *refs),
        in_specs=[smem, smem, vmem, vmem, vmem, vmem, vmem] + [vmem] * 4,
        out_specs=[vmem] * 4,
        out_shape=[*state, acc_shape],
        input_output_aliases={7: 0, 8: 1, 9: 2, 10: 3},
        compiler_params=params(8),
        cost_estimate=cost(3, 8, rows * H * 3 // 8),
        name="middle",
    )(src, dst, feats, adj, pw, wcat, bias, *held)

    if slabs > 2:
        cots.append(pair)
    for b in range(2, slabs.bit_length() - 1):
        cots.append(exchange(jnp.concatenate(cots, axis=0), "graph", 1 << b))

    order = bit_order(slabs)
    a_all, _, slope_all, p_all, fine, c_send, c_keep = pl.pallas_call(
        lambda *refs: last_kernel(three, order, *refs),
        in_specs=[smem, smem, vmem, vmem, vmem, vmem, vmem, vmem, vmem, vmem]
        + [vmem] * 4,
        out_specs=[vmem] * 4 + [hbm] + [vmem] * 2,
        out_shape=[
            *state,
            shape(slabs * TILE, 2 * H, dtype=BF16),
            row_shape,
            shape(slabs // 2, TILE, H, dtype=BF16),
            shape(slabs // 2, TILE, H),
        ],
        scratch_shapes=[
            pltpu.VMEM((slabs, TILE, H), F32),
            pltpu.VMEM((slabs, TILE, H), F32),
            pltpu.VMEM((2 * (QUAD + 2 * HT) * TILE, H), BF16),
            pltpu.VMEM((2 * H, 2 * H), BF16),
            pltpu.VMEM((rows, H), BF16),
            pltpu.SemaphoreType.DMA((count // QUAD,)),
        ],
        input_output_aliases={10: 0, 11: 1, 12: 2},
        compiler_params=params(16),
        cost_estimate=cost(4, 8, rows * H // 4),
        name="last",
    )(src, dst, near, far, feats, adj, pw, wcat, bias, w_out, *held)
    c_got = exchange(c_send, "graph", 1)

    every = cots
    keep, send = pl.pallas_call(
        lambda *refs: backward_kernel(len(every), *refs),
        in_specs=[smem]
        + [vmem] * len(every)
        + [vmem] * 5
        + [vmem],
        out_specs=[vmem, vmem],
        out_shape=[shape(PACK + 8, H)] * 2,
        scratch_shapes=[
            pltpu.VMEM((slabs * TILE, H), BF16),
            pltpu.VMEM((slabs, H, TILE), BF16),
            pltpu.VMEM((H, 2 * H), F32),
            pltpu.VMEM((H, 2 * H), F32),
            pltpu.VMEM((3, H, H), F32),
        ],
        compiler_params=params(16),
        cost_estimate=cost(3, 4),
        name="backward",
    )(dst, *every, feats, a_all, slope_all, pw, p_all, w_out)

    held = c_keep + c_got.astype(F32)
    mask = 2
    while mask < slabs:
        size = held.shape[0] // 2
        got = exchange(held[size:].astype(BF16), "graph", mask)
        held = held[:size] + got.astype(F32)
        mask *= 2
    coarse = held[0].astype(BF16)

    rounds = [("design", 1 << b) for b in range(1, designs.bit_length() - 1)]
    rounds += [("graph", 1 << b) for b in range(slabs.bit_length() - 1)]
    mine = keep + exchange(send, "design", 1)
    for n, (axis, mask) in enumerate(rounds):
        if n < len(rounds) - LOW_ROUNDS:
            mine = mine + exchange(mine, axis, mask)
        else:
            low = mine.astype(BF16)
            mine = low.astype(F32) + exchange(low, axis, mask).astype(F32)
    other = exchange(mine, "design", 1)
    scale = 1.0 / math.sqrt(designs * rows * slabs)
    g_msg, g_in, g_bias, g_out = pl.pallas_call(
        lambda *refs: finish_kernel(scale, *refs),
        in_specs=[vmem] * 4,
        out_specs=[vmem] * 4,
        out_shape=[shape(H, H), shape(2 * H, H), shape(1, H), shape(H, H)],
        scratch_shapes=[pltpu.VMEM((3, H, H), F32)],
        compiler_params=params(4),
        name="finish",
    )(mine, other, w_msg, w_in)
    return fine[None], coarse[None], g_msg, g_in, g_bias.reshape(H), g_out


def solution(mesh):
    in_specs = (
        P("design", "graph", None),
        P("design", "graph", None, None, None),
        P("design", "graph", None),
        P("design", "graph", None),
        P("design", "graph", None, None),
        P("design", "graph", None),
        P(),
        P(),
        P(),
        P(),
    )
    out_specs = (P("design", "graph", None), P("design", "graph", None), P(), P(), P(), P())
    return jax.shard_map(layer, mesh=mesh, in_specs=in_specs, out_specs=out_specs, check_vma=False)
```

```python
import math

import jax
import jax.numpy as jnp
from jax import lax
from jax.experimental import pallas as pl
from jax.experimental.pallas import tpu as pltpu
from jax.sharding import PartitionSpec as P


H = 128
TILE = 128
NBR = 4
HT = 2
QUAD = 4
F32 = jnp.float32
BF16 = jnp.bfloat16
MARGIN = HT * TILE
HALF = H // 2
PACK = 3 * HALF
LOW_ROUNDS = 1


def dot(a, b, ca=1, cb=0):
    return lax.dot_general(a, b, (((ca,), (cb,)), ((), ())), preferred_element_type=F32)


def split(x):
    hi = x.astype(BF16)
    return hi, (x - hi.astype(F32)).astype(BF16)


def diagonal(a, b):
    top = jnp.concatenate([a, jnp.zeros(b.shape, b.dtype)], axis=1)
    low = jnp.concatenate([jnp.zeros(a.shape, a.dtype), b], axis=1)
    return jnp.concatenate([top, low], axis=0)


def beside(a, b):
    return jnp.concatenate([a, b], axis=1)


def halving_order(masks):
    order = [0]
    for mask in reversed(masks):
        order = order + [r + mask for r in order]
    return order


def exchange(x, axis, mask):
    return lax.ppermute(x, axis, [(i, i ^ mask) for i in range(lax.axis_size(axis))])


def narrow(x, fine):
    high = lax.reduce_precision(x, exponent_bits=8, mantissa_bits=7)
    parts = [high.astype(BF16)]
    if fine:
        parts.append((x - high)[2 * HALF :].astype(BF16))
    return jnp.concatenate(parts, axis=0)


def widen(low):
    rows = PACK + 8
    x = low[:rows].astype(F32)
    if low.shape[0] > rows:
        rest = jnp.zeros((2 * HALF, H), F32)
        x = x + jnp.concatenate([rest, low[rows:].astype(F32)], axis=0)
    return x


def rows_at(tile, count=1):
    if isinstance(tile, int):
        return pl.ds(tile * TILE, count * TILE)
    return pl.ds(pl.multiple_of(tile * TILE, TILE), count * TILE)


def pack_kernel(nodes, cot, own, near, far, sem):
    odd = lax.axis_index("graph") & 1
    gap = nodes.shape[0] - MARGIN
    near_at = pl.multiple_of((1 - odd) * gap, TILE)
    far_at = pl.multiple_of(odd * gap, TILE)
    copies = [
        pltpu.make_async_copy(cot, own, sem.at[0]),
        pltpu.make_async_copy(nodes.at[pl.ds(near_at, MARGIN)], near, sem.at[1]),
        pltpu.make_async_copy(nodes.at[pl.ds(far_at, MARGIN)], far, sem.at[2]),
    ]
    for copy in copies:
        copy.start()
    for copy in copies:
        copy.wait()


def join_weights(w_msg, w_in, wcat):
    wcat[:H] = (0.5 * w_in[:H].astype(F32)).astype(BF16)
    wcat[H:] = (0.5 * dot(w_msg[...], w_in[H:])).astype(BF16)


def shares(quads):
    order = sorted(range(quads), key=lambda q: abs(2 * q - quads + 1))
    one, two = quads * 3 // 8, quads * 6 // 8
    return sorted(order[:one]), sorted(order[one:two]), sorted(order[two:])


def run_stages(count, *stages):
    held = {}
    for tick in range(count + len(stages) - 1):
        for k, stage in enumerate(stages):
            i = tick - k
            if 0 <= i < count:
                held[k, i] = stage(i, held.get((k - 1, i)))


def forward_quads(quads, src, dst, nodes, adj, pw, wcat, bias, outs, acc, edges=None):
    a_out, act_out, slope_out = outs
    me = lax.axis_index("graph")
    h_bias = 0.5 * bias[...]
    total = slope_out.shape[0]
    ends = {0: 0, total // QUAD - 1: 2 * (QUAD + 2 * HT) - total - 2 * HT}

    def gather(i, _):
        sums = []
        for j in range(QUAD):
            t = quads[i] * QUAD + j
            held, shift = (edges, ends[quads[i]]) if quads[i] in ends else (nodes, -HT)
            picked = [held[rows_at(src[k, t] + shift), :] for k in range(NBR)]
            weights = jnp.concatenate([adj[t, k] for k in range(NBR)], axis=1)
            sums.append(dot(weights, jnp.concatenate(picked, axis=0)).astype(BF16))
        summed = jnp.concatenate(sums, axis=0)
        a_out[rows_at(quads[i] * QUAD, QUAD), :] = summed
        return summed

    def activate(i, summed):
        first = quads[i] * QUAD
        own = nodes[rows_at(first, QUAD), :]
        h = dot(beside(own, summed), wcat[...]) + h_bias
        s = jnp.tanh(h)
        hs = h * s
        act = (h + hs).astype(BF16)
        act_out[rows_at(first, QUAD), :] = act
        slope = (1.0 + s) * ((1.0 + h) - hs)
        for j in range(QUAD):
            slope_out[first + j] = slope[j * TILE : (j + 1) * TILE].T
        return act

    def pool(i, act):
        add_pooled(quads[i] * QUAD, act, dst, me, pw, acc)

    run_stages(len(quads), gather, activate, pool)


def add_pooled(first, values, dst, me, pw, acc):
    for j in range(0, QUAD, 2):
        a, b = values[j * TILE : (j + 1) * TILE], values[(j + 1) * TILE : (j + 2) * TILE]
        t = first + j
        term = dot(beside(pw[t], pw[t + 1]), diagonal(a, b))
        acc[dst[0, t] ^ me] += term[:, :H]
        acc[dst[0, t + 1] ^ me] += term[:, H:]


def start_kernel(
    quads, src, dst, nodes, adj, pw, w_msg, w_in, bias, a_out, act_out, slope_out, acc, wcat
):
    join_weights(w_msg, w_in, wcat)
    acc[...] = jnp.zeros_like(acc)
    outs = (a_out, act_out, slope_out)
    forward_quads(quads, src, dst, nodes, adj, pw, wcat, bias, outs, acc)


def middle_kernel(
    quads, src, dst, nodes, adj, pw, wcat, bias, a_in, act_in, slope_in, acc_in,
    a_out, act_out, slope_out, acc,
):
    outs = (a_out, act_out, slope_out)
    forward_quads(quads, src, dst, nodes, adj, pw, wcat, bias, outs, acc)


def last_kernel(
    quads, src, dst, near, far, nodes, adj, pw, wcat, bias,
    a_in, act_in, slope_in, acc_in,
    a_out, act_out, slope_out, p_out, acc, edges,
):
    me = lax.axis_index("graph")
    odd = me & 1
    size = edges.shape[0]
    span = size // 2 - MARGIN
    edges[MARGIN : MARGIN + span] = nodes[:span]
    edges[size - MARGIN - span : size - MARGIN] = nodes[nodes.shape[0] - span :]
    edges[pl.ds(pl.multiple_of((1 - odd) * (size - MARGIN), TILE), MARGIN), :] = near[...]
    at_end = (me == 0) | (me == lax.axis_size("graph") - 1)
    edges[pl.ds(pl.multiple_of(odd * (size - MARGIN), TILE), MARGIN), :] = jnp.where(
        at_end, jnp.zeros_like(far), far[...]
    )
    acc[...] = acc_in[...]
    outs = (a_out, act_out, slope_out)
    forward_quads(quads, src, dst, nodes, adj, pw, wcat, bias, outs, acc, edges)
    for r in range(acc.shape[0]):
        hi, lo = split(acc[r])
        p_out[r * TILE : (r + 1) * TILE, :H] = hi
        p_out[r * TILE : (r + 1) * TILE, H:] = lo


def tail_kernel(
    order, dst, nodes, act_in, pw, w_out, fine, send, keep, pooled, wdiag, out_v, sem
):
    me = lax.axis_index("graph")
    wdiag[...] = diagonal(w_out[...], w_out[...])
    pooled[...] = jnp.zeros_like(pooled)
    half = QUAD * TILE // 2
    count = nodes.shape[0] // (QUAD * TILE)
    copies = []

    def project(i, _):
        act = act_in[rows_at(i * QUAD, QUAD), :]
        return dot(beside(act[:half], act[half:]), wdiag[...])

    def update(i, delta):
        part = rows_at(i * QUAD, QUAD)
        own = nodes[part, :].astype(F32)
        out = jnp.concatenate([own[:half] + delta[:, :H], own[half:] + delta[:, H:]], axis=0)
        out = out.astype(BF16)
        out_v[part, :] = out
        copies.append(pltpu.make_async_copy(out_v.at[part], fine.at[part], sem.at[i]))
        copies[-1].start()
        return out

    def pool(i, out):
        add_pooled(i * QUAD, out, dst, me, pw, pooled)

    run_stages(count, project, update, pool)
    slabs = len(order)
    for q, r in enumerate(order):
        if q < slabs // 2:
            keep[q] = pooled[r]
        else:
            send[q - slabs // 2] = pooled[r].astype(BF16)
    for copy in copies:
        copy.wait()


def backward_kernel(places, dst, *refs):
    pieces = len(places)
    cots = refs[:pieces]
    (nodes, a_in, slope_in, pw, p_in, w_out) = refs[pieces : pieces + 6]
    keep, send, cot_all, cot_w, total, bias, mats = refs[pieces + 6 :]
    me = lax.axis_index("graph")
    core = lax.axis_index("design") & 1
    for cot, spots in zip(cots, places):
        for n, r in enumerate(spots):
            cot_all[r * TILE : (r + 1) * TILE] = cot[n * TILE : (n + 1) * TILE]
    for r in range(cot_w.shape[0]):
        tile = cot_all[r * TILE : (r + 1) * TILE]
        cot_w[r] = (0.5 * dot(w_out[...], tile, 1, 1)).astype(BF16)
    both = dot(cot_all[...], p_in[...], 0, 0)
    mats[0] = both[:, :H] + both[:, H:]
    total[...] = jnp.zeros_like(total)
    bias[...] = jnp.zeros_like(bias)

    firsts = list(range(0, slope_in.shape[0], QUAD))

    def unpool(i, _):
        parts = []
        for j in range(0, QUAD, 2):
            t = firsts[i] + j
            left = beside(cot_w[dst[0, t] ^ me], cot_w[dst[0, t + 1] ^ me])
            parts.append(dot(left, diagonal(pw[t], pw[t + 1])))
        return parts

    def slopes(i, parts):
        done = []
        for j, part in enumerate(parts):
            t = firsts[i] + 2 * j
            grad = part * beside(slope_in[t], slope_in[t + 1])
            bias[...] += grad
            done.append(grad.astype(BF16))
        return jnp.concatenate(done, axis=1)

    def weights(i, grad_pre):
        own = nodes[rows_at(firsts[i], QUAD), :]
        total[...] += dot(grad_pre, beside(own, a_in[rows_at(firsts[i], QUAD), :]))

    run_stages(len(firsts), unpool, slopes, weights)

    mats[1] = total[:, :H]
    mats[2] = total[:, H:]
    column = jnp.sum(bias[...], axis=1, keepdims=True)
    row = jnp.broadcast_to(column, (H, H)).T[:8]
    for out, half in ((keep, core), (send, 1 - core)):
        for m in range(3):
            at = pl.multiple_of(half * HALF, HALF)
            out[m * HALF : (m + 1) * HALF] = mats[m, pl.ds(at, HALF), :]
        out[PACK:] = row


def finish_kernel(scale, held, other, w_msg, w_in, g_msg, g_in, g_bias, g_out, mats):
    core = lax.axis_index("design") & 1
    for part, half in ((held, core), (other, 1 - core)):
        for m in range(3):
            at = pl.multiple_of(half * HALF, HALF)
            mats[m, pl.ds(at, HALF), :] = part[m * HALF : (m + 1) * HALF] * scale
    g_out[...] = mats[0].T
    g_in[:H] = mats[1].T
    hi, lo = split(mats[2])
    g_in[H:] = dot(w_msg[...], hi, 0, 1) + dot(w_msg[...], lo, 0, 1)
    w_low = w_in[H:]
    g_msg[...] = dot(hi, w_low, 0, 1) + dot(lo, w_low, 0, 1)
    g_bias[...] = jnp.where(core == 0, held[PACK : PACK + 1], other[PACK : PACK + 1]) * scale


def layer(
    nodes, adjacency, tile_src, pool_dst, pool_weight, coarse_cot, w_msg, w_in, b_in, w_out
):
    def stay(x):
        return pltpu.with_memory_space_constraint(x, pltpu.HBM)

    feats = nodes[0]
    adj = adjacency[0]
    src = tile_src[0].T
    dst = pool_dst[0].T
    pw = pool_weight[0]
    cot = coarse_cot[0]
    rows = feats.shape[0]
    count = rows // TILE
    slabs = lax.axis_size("graph")
    designs = lax.axis_size("design")
    assert slabs & (slabs - 1) == 0 and designs & (designs - 1) == 0
    assert slabs > 1 and designs > 1
    assert count % (8 * QUAD) == 0
    one, two, three = shares(count // QUAD)
    bias = b_in.reshape(1, H)

    smem = pl.BlockSpec(memory_space=pltpu.SMEM)
    vmem = pl.BlockSpec(memory_space=pltpu.VMEM)
    hbm = pl.BlockSpec(memory_space=pl.ANY)

    def shape(*dims, dtype=F32):
        return jax.ShapeDtypeStruct(dims, dtype)

    def params(mib):
        return pltpu.CompilerParams(vmem_limit_bytes=mib * 1024 * 1024)

    def cost(units, mib, trans=0):
        return pl.CostEstimate(
            flops=2 * units * rows * H * H,
            bytes_accessed=mib * 1024 * 1024,
            transcendentals=trans,
        )

    bits = slabs.bit_length() - 1
    masks = [1 << b for b in range(2, bits)] + [1 << b for b in range(min(bits, 2))]
    pieces, places = [cot], [[0]]

    def gather(mask):
        sent = pieces[0] if len(pieces) == 1 else jnp.concatenate(pieces, axis=0)
        got = exchange(sent, "graph", mask)
        known = [r ^ mask for spots in places for r in spots]
        pieces.append(got)
        places.append(known)

    gather(masks[0])
    own_cot, near_send, far_send = pl.pallas_call(
        pack_kernel,
        in_specs=[hbm, hbm],
        out_specs=[vmem] * 3,
        out_shape=[shape(TILE, H, dtype=BF16)] + [shape(MARGIN, H, dtype=BF16)] * 2,
        scratch_shapes=[pltpu.SemaphoreType.DMA((3,))],
        compiler_params=params(1),
        cost_estimate=cost(40, 40),
        name="pack",
    )(stay(feats), stay(cot))
    pieces[0] = own_cot
    cross = {}
    for d in range(designs):
        for g in range(slabs):
            beyond = g + 1 if g % 2 else g - 1
            inside = 0 <= beyond < slabs
            cross[d * slabs + g] = d * slabs + beyond if inside else (d ^ 1) * slabs + g
    far = lax.ppermute(far_send, ("design", "graph"), list(cross.items()))
    near = exchange(near_send, "graph", 1)
    for mask in masks[1:]:
        if mask > 2:
            gather(mask)
    if masks[0] > 1:
        gather(1)

    row_shape = shape(rows, H, dtype=BF16)
    slope_shape = shape(count, H, TILE)
    acc_shape = shape(slabs, TILE, H)
    wcat_shape = shape(2 * H, H, dtype=BF16)
    state = [row_shape, row_shape, slope_shape]

    *held, wcat = pl.pallas_call(
        lambda *refs: start_kernel(one, *refs),
        in_specs=[smem, smem, vmem, vmem, vmem, vmem, vmem, vmem],
        out_specs=[vmem] * 5,
        out_shape=[*state, acc_shape, wcat_shape],
        compiler_params=params(8),
        cost_estimate=cost(3, 8, rows * H * 3 // 8),
        name="start",
    )(src, dst, feats, adj, pw, w_msg, w_in, bias)

    if slabs > 2:
        gather(2)

    held = pl.pallas_call(
        lambda *refs: middle_kernel(two, *refs),
        in_specs=[smem, smem, vmem, vmem, vmem, vmem, vmem] + [vmem] * 4,
        out_specs=[vmem] * 4,
        out_shape=[*state, acc_shape],
        input_output_aliases={7: 0, 8: 1, 9: 2, 10: 3},
        compiler_params=params(8),
        cost_estimate=cost(3, 8, rows * H * 3 // 8),
        name="middle",
    )(src, dst, feats, adj, pw, wcat, bias, *held)

    a_all, act_all, slope_all, p_all = pl.pallas_call(
        lambda *refs: last_kernel(three, *refs),
        in_specs=[smem, smem] + [vmem] * 11,
        out_specs=[vmem] * 4,
        out_shape=[*state, shape(slabs * TILE, 2 * H, dtype=BF16)],
        scratch_shapes=[
            pltpu.VMEM((slabs, TILE, H), F32),
            pltpu.VMEM((2 * (QUAD + 2 * HT) * TILE, H), BF16),
        ],
        input_output_aliases={9: 0, 10: 1, 11: 2},
        compiler_params=params(8),
        cost_estimate=cost(2, 4, rows * H // 4),
        name="last",
    )(src, dst, near, far, feats, adj, pw, wcat, bias, *held)

    keep, send = pl.pallas_call(
        lambda *refs: backward_kernel(places, *refs),
        in_specs=[smem]
        + [vmem] * len(pieces)
        + [vmem] * 5
        + [vmem],
        out_specs=[vmem, vmem],
        out_shape=[shape(PACK + 8, H)] * 2,
        scratch_shapes=[
            pltpu.VMEM((slabs * TILE, H), BF16),
            pltpu.VMEM((slabs, H, TILE), BF16),
            pltpu.VMEM((H, 2 * H), F32),
            pltpu.VMEM((H, 2 * H), F32),
            pltpu.VMEM((3, H, H), F32),
        ],
        compiler_params=params(16),
        cost_estimate=cost(3, 4),
        name="backward",
    )(dst, *pieces, feats, a_all, slope_all, pw, p_all, w_out)

    halving = [2, 1] + masks[:-2] if slabs > 2 else masks
    order = halving_order(halving)
    fine, c_send, held = pl.pallas_call(
        lambda *refs: tail_kernel(order, *refs),
        in_specs=[smem] + [vmem] * 4,
        out_specs=[hbm, vmem, vmem],
        out_shape=[
            row_shape,
            shape(slabs // 2, TILE, H, dtype=BF16),
            shape(slabs // 2, TILE, H),
        ],
        scratch_shapes=[
            pltpu.VMEM((slabs, TILE, H), F32),
            pltpu.VMEM((2 * H, 2 * H), BF16),
            pltpu.VMEM((rows, H), BF16),
            pltpu.SemaphoreType.DMA((count // QUAD,)),
        ],
        compiler_params=params(12),
        cost_estimate=cost(2, 4),
        name="tail",
    )(dst, feats, act_all, pw, w_out)
    for mask in halving:
        held = held + exchange(c_send, "graph", mask).astype(F32)
        size = held.shape[0] // 2
        held, c_send = held[:size] if size else held, held[size:].astype(BF16)
    coarse = held[0].astype(BF16)

    rounds = [("design", 1 << b) for b in range(1, designs.bit_length() - 1)]
    rounds += [("graph", 1 << b) for b in range(slabs.bit_length() - 1)]
    mine = keep + exchange(send, "design", 1)
    for n, (axis, mask) in enumerate(rounds):
        low = narrow(mine, n < len(rounds) - LOW_ROUNDS)
        mine = widen(low) + widen(exchange(low, axis, mask))
    other = exchange(mine, "design", 1)
    scale = 1.0 / math.sqrt(designs * rows * slabs)
    g_msg, g_in, g_bias, g_out = pl.pallas_call(
        lambda *refs: finish_kernel(scale, *refs),
        in_specs=[vmem] * 4,
        out_specs=[vmem] * 4,
        out_shape=[shape(H, H), shape(2 * H, H), shape(1, H), shape(H, H)],
        scratch_shapes=[pltpu.VMEM((3, H, H), F32)],
        compiler_params=params(4),
        name="finish",
    )(mine, other, w_msg, w_in)
    return fine[None], coarse[None], g_msg, g_in, g_bias.reshape(H), g_out


def solution(mesh):
    in_specs = (
        P("design", "graph", None),
        P("design", "graph", None, None, None),
        P("design", "graph", None),
        P("design", "graph", None),
        P("design", "graph", None, None),
        P("design", "graph", None),
        P(),
        P(),
        P(),
        P(),
    )
    out_specs = (P("design", "graph", None), P("design", "graph", None), P(), P(), P(), P())
    return jax.shard_map(layer, mesh=mesh, in_specs=in_specs, out_specs=out_specs, check_vma=False)
```

```python
import math

import jax
import jax.numpy as jnp
from jax import lax
from jax.experimental import pallas as pl
from jax.experimental.pallas import tpu as pltpu
from jax.sharding import PartitionSpec as P


H = 128
TILE = 128
NBR = 4
HT = 2
QUAD = 4
F32 = jnp.float32
BF16 = jnp.bfloat16
MARGIN = HT * TILE
HALF = H // 2
PACK = 3 * HALF
LOW_ROUNDS = 2


def dot(a, b, ca=1, cb=0):
    return lax.dot_general(a, b, (((ca,), (cb,)), ((), ())), preferred_element_type=F32)


def split(x):
    hi = x.astype(BF16)
    return hi, (x - hi.astype(F32)).astype(BF16)


def diagonal(a, b):
    top = jnp.concatenate([a, jnp.zeros(b.shape, b.dtype)], axis=1)
    low = jnp.concatenate([jnp.zeros(a.shape, a.dtype), b], axis=1)
    return jnp.concatenate([top, low], axis=0)


def beside(a, b):
    return jnp.concatenate([a, b], axis=1)


def halving_order(masks):
    order = [0]
    for mask in reversed(masks):
        order = order + [r + mask for r in order]
    return order


def swap_low(x):
    return (x & ~3) | ((x & 1) << 1) | ((x >> 1) & 1)


def exchange(x, moves):
    designs, slabs = lax.axis_size("design"), lax.axis_size("graph")
    pairs = []
    for d in range(designs):
        axis, mask = moves[d & 1]
        for g in range(slabs):
            to = (d ^ mask, g) if axis == "design" else (d, g ^ mask)
            pairs.append((d * slabs + g, to[0] * slabs + to[1]))
    return lax.ppermute(x, ("design", "graph"), pairs)


def both(axis, mask):
    return (axis, mask), (axis, mask)


def steps(mask):
    return ("graph", mask), ("graph", swap_low(mask) if lax.axis_size("graph") > 2 else mask)


def slot_of(dst, tile):
    x = dst[0, tile] ^ lax.axis_index("graph")
    if lax.axis_size("graph") == 2:
        return x
    return jnp.where(lax.axis_index("design") & 1 == 1, swap_low(x), x)


def narrow(x, fine):
    high = lax.reduce_precision(x, exponent_bits=8, mantissa_bits=7)
    parts = [high.astype(BF16)]
    if fine:
        parts.append((x - high)[2 * HALF :].astype(BF16))
    return jnp.concatenate(parts, axis=0)


def widen(low):
    rows = PACK + 8
    x = low[:rows].astype(F32)
    if low.shape[0] > rows:
        rest = jnp.zeros((2 * HALF, H), F32)
        x = x + jnp.concatenate([rest, low[rows:].astype(F32)], axis=0)
    return x


def rows_at(tile, count=1):
    if isinstance(tile, int):
        return pl.ds(tile * TILE, count * TILE)
    return pl.ds(pl.multiple_of(tile * TILE, TILE), count * TILE)


def pack_kernel(nodes, cot, own, near, far, sem):
    odd = lax.axis_index("graph") & 1
    gap = nodes.shape[0] - MARGIN
    near_at = pl.multiple_of((1 - odd) * gap, TILE)
    far_at = pl.multiple_of(odd * gap, TILE)
    copies = [
        pltpu.make_async_copy(cot, own, sem.at[0]),
        pltpu.make_async_copy(nodes.at[pl.ds(near_at, MARGIN)], near, sem.at[1]),
        pltpu.make_async_copy(nodes.at[pl.ds(far_at, MARGIN)], far, sem.at[2]),
    ]
    for copy in copies:
        copy.start()
    for copy in copies:
        copy.wait()


def join_weights(w_msg, w_in, wcat):
    wcat[:H] = (0.5 * w_in[:H].astype(F32)).astype(BF16)
    wcat[H:] = (0.5 * dot(w_msg[...], w_in[H:])).astype(BF16)


def shares(quads):
    order = sorted(range(quads), key=lambda q: abs(2 * q - quads + 1))
    cut = quads * 3 // 8
    return sorted(order[:cut]), sorted(order[cut:], key=lambda q: q in (0, quads - 1))


def run_stages(count, *stages):
    held = {}
    for tick in range(count + len(stages) - 1):
        for k, stage in enumerate(stages):
            i = tick - k
            if 0 <= i < count:
                held[k, i] = stage(i, held.get((k - 1, i)))


def forward_quads(quads, src, dst, nodes, adj, pw, wcat, bias, outs, acc, edges=None):
    a_out, act_out, slope_out = outs
    h_bias = 0.5 * bias[...]
    total = slope_out.shape[0]
    ends = {0: 0, total // QUAD - 1: 2 * (QUAD + 2 * HT) - total - 2 * HT}

    def gather(i, _):
        sums = []
        for j in range(QUAD):
            t = quads[i] * QUAD + j
            held, shift = (edges, ends[quads[i]]) if quads[i] in ends else (nodes, -HT)
            picked = [held[rows_at(src[k, t] + shift), :] for k in range(NBR)]
            weights = jnp.concatenate([adj[t, k] for k in range(NBR)], axis=1)
            sums.append(dot(weights, jnp.concatenate(picked, axis=0)).astype(BF16))
        summed = jnp.concatenate(sums, axis=0)
        a_out[rows_at(quads[i] * QUAD, QUAD), :] = summed
        return summed

    def activate(i, summed):
        first = quads[i] * QUAD
        own = nodes[rows_at(first, QUAD), :]
        h = dot(beside(own, summed), wcat[...]) + h_bias
        s = jnp.tanh(h)
        hs = h * s
        act = (h + hs).astype(BF16)
        act_out[rows_at(first, QUAD), :] = act
        slope = (1.0 + s) * ((1.0 + h) - hs)
        for j in range(QUAD):
            slope_out[first + j] = slope[j * TILE : (j + 1) * TILE].T
        return act

    def pool(i, act):
        add_pooled(quads[i] * QUAD, act, lambda t: slot_of(dst, t), pw, acc)

    run_stages(len(quads), gather, activate, pool)


def add_pooled(first, values, slots, pw, acc):
    for j in range(0, QUAD, 2):
        a, b = values[j * TILE : (j + 1) * TILE], values[(j + 1) * TILE : (j + 2) * TILE]
        t = first + j
        term = dot(beside(pw[t], pw[t + 1]), diagonal(a, b))
        acc[slots(t)] += term[:, :H]
        acc[slots(t + 1)] += term[:, H:]


def start_kernel(
    quads, src, dst, nodes, adj, pw, w_msg, w_in, bias, a_out, act_out, slope_out, acc, wcat
):
    join_weights(w_msg, w_in, wcat)
    acc[...] = jnp.zeros_like(acc)
    outs = (a_out, act_out, slope_out)
    forward_quads(quads, src, dst, nodes, adj, pw, wcat, bias, outs, acc)


def last_kernel(
    quads, src, dst, near, far, nodes, adj, pw, wcat, bias,
    a_in, act_in, slope_in, acc_in,
    a_out, act_out, slope_out, p_out, acc, edges,
):
    me = lax.axis_index("graph")
    odd = me & 1
    size = edges.shape[0]
    span = size // 2 - MARGIN
    edges[MARGIN : MARGIN + span] = nodes[:span]
    edges[size - MARGIN - span : size - MARGIN] = nodes[nodes.shape[0] - span :]
    edges[pl.ds(pl.multiple_of((1 - odd) * (size - MARGIN), TILE), MARGIN), :] = near[...]
    at_end = (me == 0) | (me == lax.axis_size("graph") - 1)
    edges[pl.ds(pl.multiple_of(odd * (size - MARGIN), TILE), MARGIN), :] = jnp.where(
        at_end, jnp.zeros_like(far), far[...]
    )
    acc[...] = acc_in[...]
    outs = (a_out, act_out, slope_out)
    forward_quads(quads, src, dst, nodes, adj, pw, wcat, bias, outs, acc, edges)
    for r in range(acc.shape[0]):
        hi, lo = split(acc[r])
        p_out[r * TILE : (r + 1) * TILE, :H] = hi
        p_out[r * TILE : (r + 1) * TILE, H:] = lo


def tail_kernel(
    order, dst, nodes, act_in, pw, w_out, fine, send, keep, pooled, wdiag, out_v, sem
):
    me = lax.axis_index("graph")
    wdiag[...] = diagonal(w_out[...], w_out[...])
    pooled[...] = jnp.zeros_like(pooled)
    half = QUAD * TILE // 2
    count = nodes.shape[0] // (QUAD * TILE)
    copies = []

    def project(i, _):
        act = act_in[rows_at(i * QUAD, QUAD), :]
        return dot(beside(act[:half], act[half:]), wdiag[...])

    def update(i, delta):
        part = rows_at(i * QUAD, QUAD)
        own = nodes[part, :].astype(F32)
        out = jnp.concatenate([own[:half] + delta[:, :H], own[half:] + delta[:, H:]], axis=0)
        out = out.astype(BF16)
        out_v[part, :] = out
        copies.append(pltpu.make_async_copy(out_v.at[part], fine.at[part], sem.at[i]))
        copies[-1].start()
        return out

    def pool(i, out):
        add_pooled(i * QUAD, out, lambda t: dst[0, t] ^ me, pw, pooled)

    run_stages(count, project, update, pool)
    slabs = len(order)
    for q, r in enumerate(order):
        if q < slabs // 2:
            keep[q] = pooled[r]
        else:
            send[q - slabs // 2] = pooled[r].astype(BF16)
    for copy in copies:
        copy.wait()


def backward_kernel(places, dst, *refs):
    pieces = len(places)
    cots = refs[:pieces]
    (nodes, a_in, slope_in, pw, p_in, w_out) = refs[pieces : pieces + 6]
    keep, send, cot_all, cot_w, total, bias, mats = refs[pieces + 6 :]
    core = lax.axis_index("design") & 1
    for cot, spots in zip(cots, places):
        for n, r in enumerate(spots):
            cot_all[r * TILE : (r + 1) * TILE] = cot[n * TILE : (n + 1) * TILE]
    for r in range(cot_w.shape[0]):
        tile = cot_all[r * TILE : (r + 1) * TILE]
        cot_w[r] = (0.5 * dot(w_out[...], tile, 1, 1)).astype(BF16)
    both = dot(cot_all[...], p_in[...], 0, 0)
    mats[0] = both[:, :H] + both[:, H:]
    total[...] = jnp.zeros_like(total)
    bias[...] = jnp.zeros_like(bias)

    firsts = list(range(0, slope_in.shape[0], QUAD))

    def unpool(i, _):
        parts = []
        for j in range(0, QUAD, 2):
            t = firsts[i] + j
            left = beside(cot_w[slot_of(dst, t)], cot_w[slot_of(dst, t + 1)])
            parts.append(dot(left, diagonal(pw[t], pw[t + 1])))
        return parts

    def slopes(i, parts):
        done = []
        for j, part in enumerate(parts):
            t = firsts[i] + 2 * j
            grad = part * beside(slope_in[t], slope_in[t + 1])
            bias[...] += grad
            done.append(grad.astype(BF16))
        return jnp.concatenate(done, axis=1)

    def weights(i, grad_pre):
        own = nodes[rows_at(firsts[i], QUAD), :]
        total[...] += dot(grad_pre, beside(own, a_in[rows_at(firsts[i], QUAD), :]))

    run_stages(len(firsts), unpool, slopes, weights)

    mats[1] = total[:, :H]
    mats[2] = total[:, H:]
    column = jnp.sum(bias[...], axis=1, keepdims=True)
    row = jnp.broadcast_to(column, (H, H)).T[:8]
    for out, half in ((keep, core), (send, 1 - core)):
        for m in range(3):
            at = pl.multiple_of(half * HALF, HALF)
            out[m * HALF : (m + 1) * HALF] = mats[m, pl.ds(at, HALF), :]
        out[PACK:] = row


def finish_kernel(
    scale, held, other, w_msg, w_in, c_held, c_got, g_msg, g_in, g_bias, g_out, coarse, mats
):
    coarse[...] = (c_held[0] + c_got[0].astype(F32)).astype(BF16)
    core = lax.axis_index("design") & 1
    for part, half in ((held, core), (other, 1 - core)):
        for m in range(3):
            at = pl.multiple_of(half * HALF, HALF)
            mats[m, pl.ds(at, HALF), :] = part[m * HALF : (m + 1) * HALF] * scale
    g_out[...] = mats[0].T
    g_in[:H] = mats[1].T
    hi, lo = split(mats[2])
    g_in[H:] = dot(w_msg[...], hi, 0, 1) + dot(w_msg[...], lo, 0, 1)
    w_low = w_in[H:]
    g_msg[...] = dot(hi, w_low, 0, 1) + dot(lo, w_low, 0, 1)
    g_bias[...] = jnp.where(core == 0, held[PACK : PACK + 1], other[PACK : PACK + 1]) * scale


def layer(
    nodes, adjacency, tile_src, pool_dst, pool_weight, coarse_cot, w_msg, w_in, b_in, w_out
):
    def stay(x):
        return pltpu.with_memory_space_constraint(x, pltpu.HBM)

    feats = nodes[0]
    adj = adjacency[0]
    src = tile_src[0].T
    dst = pool_dst[0].T
    pw = pool_weight[0]
    cot = coarse_cot[0]
    rows = feats.shape[0]
    count = rows // TILE
    slabs = lax.axis_size("graph")
    designs = lax.axis_size("design")
    assert slabs & (slabs - 1) == 0 and designs & (designs - 1) == 0
    assert slabs > 1 and designs > 1
    assert count % (8 * QUAD) == 0
    one, rest = shares(count // QUAD)
    bias = b_in.reshape(1, H)

    smem = pl.BlockSpec(memory_space=pltpu.SMEM)
    vmem = pl.BlockSpec(memory_space=pltpu.VMEM)
    hbm = pl.BlockSpec(memory_space=pl.ANY)

    def shape(*dims, dtype=F32):
        return jax.ShapeDtypeStruct(dims, dtype)

    def params(mib):
        return pltpu.CompilerParams(vmem_limit_bytes=mib * 1024 * 1024)

    def cost(units, mib, trans=0):
        return pl.CostEstimate(
            flops=2 * units * rows * H * H,
            bytes_accessed=mib * 1024 * 1024,
            transcendentals=trans,
        )

    bits = slabs.bit_length() - 1
    masks = [1 << b for b in range(2, bits)] + [1 << b for b in range(min(bits, 2))]
    pieces, places = [cot], [[0]]

    def gather(mask):
        sent = pieces[0] if len(pieces) == 1 else jnp.concatenate(pieces, axis=0)
        got = exchange(sent, steps(mask))
        known = [r ^ mask for spots in places for r in spots]
        pieces.append(got)
        places.append(known)

    gather(masks[0])
    own_cot, near_send, far_send = pl.pallas_call(
        pack_kernel,
        in_specs=[hbm, hbm],
        out_specs=[vmem] * 3,
        out_shape=[shape(TILE, H, dtype=BF16)] + [shape(MARGIN, H, dtype=BF16)] * 2,
        scratch_shapes=[pltpu.SemaphoreType.DMA((3,))],
        compiler_params=params(1),
        cost_estimate=cost(40, 40),
        name="pack",
    )(stay(feats), stay(cot))
    pieces[0] = own_cot
    cross = {}
    for d in range(designs):
        for g in range(slabs):
            beyond = g + 1 if g % 2 else g - 1
            inside = 0 <= beyond < slabs
            cross[d * slabs + g] = d * slabs + beyond if inside else (d ^ 1) * slabs + g
    far = lax.ppermute(far_send, ("design", "graph"), list(cross.items()))
    near = exchange(near_send, both("graph", 1))
    for mask in masks[1:]:
        if mask > 2:
            gather(mask)
    if masks[0] > 1:
        gather(1)

    row_shape = shape(rows, H, dtype=BF16)
    slope_shape = shape(count, H, TILE)
    acc_shape = shape(slabs, TILE, H)
    wcat_shape = shape(2 * H, H, dtype=BF16)
    state = [row_shape, row_shape, slope_shape]

    *held, wcat = pl.pallas_call(
        lambda *refs: start_kernel(one, *refs),
        in_specs=[smem, smem, vmem, vmem, vmem, vmem, vmem, vmem],
        out_specs=[vmem] * 5,
        out_shape=[*state, acc_shape, wcat_shape],
        compiler_params=params(8),
        cost_estimate=cost(3, 8, rows * H * 3 // 8),
        name="start",
    )(src, dst, feats, adj, pw, w_msg, w_in, bias)

    if slabs > 2:
        gather(2)

    a_all, act_all, slope_all, p_all = pl.pallas_call(
        lambda *refs: last_kernel(rest, *refs),
        in_specs=[smem, smem] + [vmem] * 11,
        out_specs=[vmem] * 4,
        out_shape=[*state, shape(slabs * TILE, 2 * H, dtype=BF16)],
        scratch_shapes=[
            pltpu.VMEM((slabs, TILE, H), F32),
            pltpu.VMEM((2 * (QUAD + 2 * HT) * TILE, H), BF16),
        ],
        input_output_aliases={9: 0, 10: 1, 11: 2},
        compiler_params=params(8),
        cost_estimate=cost(5, 8, rows * H * 5 // 8),
        name="last",
    )(src, dst, near, far, feats, adj, pw, wcat, bias, *held)

    keep, send = pl.pallas_call(
        lambda *refs: backward_kernel(places, *refs),
        in_specs=[smem]
        + [vmem] * len(pieces)
        + [vmem] * 5
        + [vmem],
        out_specs=[vmem, vmem],
        out_shape=[shape(PACK + 8, H)] * 2,
        scratch_shapes=[
            pltpu.VMEM((slabs * TILE, H), BF16),
            pltpu.VMEM((slabs, H, TILE), BF16),
            pltpu.VMEM((H, 2 * H), F32),
            pltpu.VMEM((H, 2 * H), F32),
            pltpu.VMEM((3, H, H), F32),
        ],
        compiler_params=params(16),
        cost_estimate=cost(3, 4),
        name="backward",
    )(dst, *pieces, feats, a_all, slope_all, pw, p_all, w_out)

    halving = [2, 1] + masks[:-2] if slabs > 2 else masks
    order = halving_order(halving)
    fine, c_send, held = pl.pallas_call(
        lambda *refs: tail_kernel(order, *refs),
        in_specs=[smem] + [vmem] * 4,
        out_specs=[hbm, vmem, vmem],
        out_shape=[
            row_shape,
            shape(slabs // 2, TILE, H, dtype=BF16),
            shape(slabs // 2, TILE, H),
        ],
        scratch_shapes=[
            pltpu.VMEM((slabs, TILE, H), F32),
            pltpu.VMEM((2 * H, 2 * H), BF16),
            pltpu.VMEM((rows, H), BF16),
            pltpu.SemaphoreType.DMA((count // QUAD,)),
        ],
        compiler_params=params(12),
        cost_estimate=cost(2, 4),
        name="tail",
    )(dst, feats, act_all, pw, w_out)
    for n, mask in enumerate(halving):
        got = exchange(c_send, both("graph", mask))
        if n < len(halving) - 1:
            size = held.shape[0] // 2
            held = held + got.astype(F32)
            held, c_send = held[:size], held[size:].astype(BF16)

    rounds = [("design", 1 << b) for b in range(1, designs.bit_length() - 1)]
    rounds += [("graph", 1 << b) for b in range(slabs.bit_length() - 1)]
    mine = keep + exchange(send, both("design", 1))
    for n, (axis, mask) in enumerate(rounds):
        low = narrow(mine, n < len(rounds) - LOW_ROUNDS)
        mine = widen(low) + widen(exchange(low, both(axis, mask)))
    other = exchange(mine, both("design", 1))
    scale = 1.0 / math.sqrt(designs * rows * slabs)
    g_msg, g_in, g_bias, g_out, coarse = pl.pallas_call(
        lambda *refs: finish_kernel(scale, *refs),
        in_specs=[vmem] * 6,
        out_specs=[vmem] * 5,
        out_shape=[
            shape(H, H), shape(2 * H, H), shape(1, H), shape(H, H), shape(TILE, H, dtype=BF16),
        ],
        scratch_shapes=[pltpu.VMEM((3, H, H), F32)],
        compiler_params=params(4),
        name="finish",
    )(mine, other, w_msg, w_in, held, got)
    return fine[None], coarse[None], g_msg, g_in, g_bias.reshape(H), g_out


def solution(mesh):
    in_specs = (
        P("design", "graph", None),
        P("design", "graph", None, None, None),
        P("design", "graph", None),
        P("design", "graph", None),
        P("design", "graph", None, None),
        P("design", "graph", None),
        P(),
        P(),
        P(),
        P(),
    )
    out_specs = (P("design", "graph", None), P("design", "graph", None), P(), P(), P(), P())
    return jax.shard_map(layer, mesh=mesh, in_specs=in_specs, out_specs=out_specs, check_vma=False)
```
